256 devices in a mesh: rep: 8 (over y, x_hi), blk: 32 (over z, x_lo, core).
Axes of the slice: x: 4 (x_hi: 2, x_lo: 2; x = x_hi * 2 + x_lo), y: 4, z: 8, core: 2. Of those that a mesh axis runs over, the one named last changes fastest.
Arguments:
- features: bfloat16 [131072, 128], P(('rep', 'blk')), may hold values from -6 to 6
- degrees: int32 [131072], P(('rep', 'blk')), may hold values from 1 to 32
- tile_weights: bfloat16 [8, 32, 320, 128, 128], P('rep', 'blk'), may hold values from 0 to 0.049804688
- tile_rows: int32 [8, 32, 320], P('rep', 'blk'), may hold values from 0 to 127, as said below
- tile_cols: int32 [8, 32, 320], P('rep', 'blk'), may hold values from 0 to 31, as said below
- tile_counts: int32 [8, 32], P('rep', 'blk'), may hold values from 1 to 320, as said below
- weight: bfloat16 [128, 256], replicated, may hold values from -0.5 to 0.5
- layer_bias: float32 [256], replicated, may hold values from -3 to 3
- upstream: bfloat16 [131072, 256], P(('rep', 'blk')), may hold values from -6 to 6
Outputs:
- hidden: bfloat16 [131072, 256], P(('rep', 'blk'))
- feature_grad: bfloat16 [131072, 128], P(('rep', 'blk'))
- weight_grad: float32 [128, 256], replicated
- bias_grad: float32 [256], replicated
The draws below stay inside these ranges and needn't reach their ends.
Inputs may be any that keep to these rules, and one draw needn't show every extreme that they name: `tile_rows`: the first tile_counts slots of a device hold distinct tiles, ordered by row and then by column; a used row h lies in node block r * 32 + h // 4, whose index h // 4 is within 3 steps of the device's blk index around the loop of 32; unused slots hold the device's own first tile row. `tile_cols`: unused slots hold 0. `tile_counts`: at most 80 used slots of one device lie in the rows of one node block; this and the largest count are both reached by some device in every draw.
All inputs are finite; a program needn't handle non-finite values.
Results may differ from the reference program's by a relative error of at most 0.015.
Values may be sent and summed in bfloat16 or wider, within the bound.
A program may use at most 128 MiB of HBM per device.

```python
import jax
import jax.numpy as jnp
from jax import lax

F = 128
HID = 256
TILE = 128
TB = 4
REACH = 3
NODES = 131072
CAPG = 80
MAXT = 320
N_REP = 8
N_BLK = 32


def tile_plan(key):
    base = jax.random.fold_in(key, 17)
    key_full, key_loss, key_order = jax.random.split(base, 3)
    device_total = N_REP * N_BLK
    group_slots = N_REP * TB * TB
    device_ids = jnp.arange(device_total, dtype=jnp.int32)
    blk_ids = device_ids % N_BLK
    group_ids = jnp.arange(N_BLK, dtype=jnp.int32)
    forward_gap = (group_ids[None, :] - blk_ids[:, None]) % N_BLK
    distance = jnp.minimum(forward_gap, N_BLK - forward_gap)
    ceiling = jnp.where(distance <= REACH, CAPG * (REACH + 1 - distance) // (REACH + 1), 0)
    full_device = jax.random.randint(key_full, (), 0, device_total)
    shortfall = jax.random.randint(key_loss, (device_total, N_BLK), 0, 1 << 20) % (ceiling // 2 + 1)
    shortfall = jnp.where(device_ids[:, None] == full_device, 0, shortfall)
    group_count = ceiling - shortfall
    slot_ids = jnp.arange(group_slots, dtype=jnp.int32)
    scores = jax.random.randint(key_order, (device_total, N_BLK, group_slots), 0, (1 << 30) // group_slots) * group_slots + slot_ids
    ranking = jnp.argsort(jnp.argsort(scores, axis=-1), axis=-1)
    chosen = ranking < group_count[:, :, None]
    place_in_group = jnp.cumsum(chosen.astype(jnp.int32), axis=-1) - 1
    group_start = jnp.cumsum(group_count, axis=-1) - group_count
    target_slot = jnp.where(chosen, group_start[:, :, None] + place_in_group, MAXT).astype(jnp.int32)
    row_value = group_ids[None, :, None] * TB + slot_ids[None, None, :] // (N_REP * TB)
    col_value = slot_ids[None, None, :] % (N_REP * TB)
    row_value = jnp.broadcast_to(row_value, chosen.shape).astype(jnp.int32)
    col_value = jnp.broadcast_to(col_value, chosen.shape).astype(jnp.int32)

    def place_slots(target, rows_in, cols_in, blk_id):
        row_array = jnp.zeros((MAXT + 1,), jnp.int32) + blk_id * TB
        col_array = jnp.zeros((MAXT + 1,), jnp.int32)
        row_array = row_array.at[target.reshape(-1)].set(rows_in.reshape(-1))
        col_array = col_array.at[target.reshape(-1)].set(cols_in.reshape(-1))
        return (row_array[:MAXT], col_array[:MAXT])
    row_table, col_table = jax.vmap(place_slots)(target_slot, row_value, col_value, blk_ids)
    counts = jnp.sum(group_count, axis=-1).astype(jnp.int32)
    return (row_table.reshape(N_REP, N_BLK, MAXT), col_table.reshape(N_REP, N_BLK, MAXT), counts.reshape(N_REP, N_BLK))


def draw_tile_rows(key, part):
    return tile_plan(key)[0]


def draw_tile_cols(key, part):
    return tile_plan(key)[1]


def draw_tile_counts(key, part):
    return tile_plan(key)[2]


def place_ends(entries, stream_key, least, largest):
    place = [jax.random.randint(jax.random.fold_in(stream_key, axis), (), 0, length) for axis, length in enumerate(entries.shape)]
    main_axis = entries.shape.index(max(entries.shape))
    neighbour = place[:main_axis] + [(place[main_axis] + 1) % entries.shape[main_axis]] + place[main_axis + 1:]
    return entries.at[tuple(place)].set(least).at[tuple(neighbour)].set(largest)


def shard_levels(own_key, dims, cuts, low, high):
    factor_of = 1.0
    for axis_at, blocks in cuts:
        heights = jax.random.uniform(jax.random.fold_in(jax.random.fold_in(own_key, 6), axis_at), (blocks,), jnp.float32, low / len(cuts), high / len(cuts))
        factor_of = factor_of * jnp.repeat(jnp.exp(heights), dims[axis_at] // blocks).reshape((-1,) + (1,) * (len(dims) - 1 - axis_at))
    return factor_of


def scatter_about(key, dims, deviation, reach, cuts=(), held_as=jnp.bfloat16):
    drawn = deviation * jax.random.normal(key, dims, jnp.float32)
    if cuts:
        drawn = drawn * shard_levels(key, dims, cuts, -0.22, 0.18)
    return jnp.clip(drawn, -reach, reach).astype(held_as)


def setup_inputs(seed: int = 0) -> dict:
    streams_of = jax.random.split(jax.random.key(seed), 10)
    return {
        "features": scatter_about(streams_of[0], (NODES, F), 1.0, 6.0, ((0, 256),)),
        "degrees": place_ends(jax.random.randint(streams_of[1], (NODES,), 1, 33), jax.random.fold_in(streams_of[1], 1), 1, 32).astype(jnp.int32),
        "tile_weights": jnp.clip(0.049804688 * jax.random.uniform(streams_of[2], (N_REP, N_BLK, MAXT, TILE, TILE), jnp.float32) ** shard_levels(streams_of[2], (N_REP, N_BLK, MAXT, TILE, TILE), ((0, 8), (1, 32)), -0.2, 0.2), 0.0, 0.049804688).astype(jnp.bfloat16),
        "tile_rows": draw_tile_rows(jax.random.fold_in(streams_of[9], 71), 0),
        "tile_cols": draw_tile_cols(jax.random.fold_in(streams_of[9], 71), 0),
        "tile_counts": draw_tile_counts(jax.random.fold_in(streams_of[9], 71), 0),
        "weight": scatter_about(streams_of[6], (F, HID), F ** -0.5, 0.5),
        "layer_bias": scatter_about(streams_of[7], (HID,), 0.5, 3.0, (), jnp.float32),
        "upstream": scatter_about(streams_of[8], (NODES, HID), 1.0, 6.0, ((0, 256),)),
    }


def node_scale(degrees):
    return 1.0 / jnp.sqrt(degrees.astype(jnp.float32) + 1.0)

def reference(features, degrees, tile_weights, tile_rows, tile_cols, tile_counts, weight, layer_bias, upstream):
    node_norm = node_scale(degrees)
    scaled = (node_norm[:, None] * features.astype(jnp.float32)).astype(jnp.bfloat16)
    tile_total = NODES // TILE
    scaled_tiles = scaled.reshape(tile_total, TILE, F)
    device_total = N_REP * N_BLK
    flat_weights = tile_weights.reshape(device_total, MAXT, TILE, TILE)
    flat_rows = tile_rows.reshape(device_total, MAXT)
    flat_cols = tile_cols.reshape(device_total, MAXT)
    flat_counts = tile_counts.reshape(device_total)
    device_ids = jnp.arange(device_total, dtype=jnp.int32)
    slot_ids = jnp.arange(MAXT, dtype=jnp.int32)

    def tile_places(row_ids, col_ids, slot_count, device):
        rep_index = device // N_BLK
        blk_index = device % N_BLK
        dest_tiles = rep_index * (N_BLK * TB) + row_ids
        source_tiles = (col_ids // TB * N_BLK + blk_index) * TB + col_ids % TB
        slot_valid = slot_ids < slot_count
        dest_tiles = jnp.where(slot_valid, dest_tiles, tile_total).astype(jnp.int32)
        source_tiles = jnp.where(slot_valid, source_tiles, tile_total).astype(jnp.int32)
        return (dest_tiles, source_tiles)

    def forward_step(running, scan_items):
        weights_dev, row_ids, col_ids, slot_count, device = scan_items
        dest_tiles, source_tiles = tile_places(row_ids, col_ids, slot_count, device)
        gathered = scaled_tiles[jnp.minimum(source_tiles, tile_total - 1)]
        products = jnp.einsum('tab,tbf->taf', weights_dev.astype(jnp.float32), gathered.astype(jnp.float32))
        return (running.at[dest_tiles].add(products), None)
    zero_sum = jnp.zeros((tile_total + 1, TILE, F), jnp.float32)
    neighbor_sum, _ = lax.scan(forward_step, zero_sum, (flat_weights, flat_rows, flat_cols, flat_counts, device_ids))
    neighbor_sum = neighbor_sum[:tile_total].reshape(NODES, F)
    aggregated = (node_norm[:, None] * (neighbor_sum + scaled.astype(jnp.float32))).astype(jnp.bfloat16)
    pre_act = jnp.dot(aggregated, weight, preferred_element_type=jnp.float32) + layer_bias
    hidden = jax.nn.silu(pre_act).astype(jnp.bfloat16)
    gate_sigmoid = jax.nn.sigmoid(pre_act)
    pre_grad = (upstream.astype(jnp.float32) * (gate_sigmoid + pre_act * gate_sigmoid * (1.0 - gate_sigmoid))).astype(jnp.bfloat16)
    grad_scale = NODES ** (-0.5)
    weight_grad = jnp.dot(aggregated.T, pre_grad, preferred_element_type=jnp.float32) * grad_scale
    bias_grad = lax.optimization_barrier(jnp.sum(pre_grad.astype(jnp.float32), axis=0)) * grad_scale
    scaled_grad = (node_norm[:, None] * jnp.dot(pre_grad, weight.T, preferred_element_type=jnp.float32)).astype(jnp.bfloat16)
    grad_tiles = scaled_grad.reshape(tile_total, TILE, F)

    def backward_step(running, scan_items):
        weights_dev, row_ids, col_ids, slot_count, device = scan_items
        dest_tiles, source_tiles = tile_places(row_ids, col_ids, slot_count, device)
        gathered = grad_tiles[jnp.minimum(dest_tiles, tile_total - 1)]
        products = jnp.einsum('tab,taf->tbf', weights_dev.astype(jnp.float32), gathered.astype(jnp.float32))
        return (running.at[source_tiles].add(products), None)
    column_sum, _ = lax.scan(backward_step, zero_sum, (flat_weights, flat_rows, flat_cols, flat_counts, device_ids))
    column_sum = column_sum[:tile_total].reshape(NODES, F)
    feature_grad = (node_norm[:, None] * (column_sum + scaled_grad.astype(jnp.float32))).astype(jnp.bfloat16)
    return (hidden, feature_grad, weight_grad, bias_grad)
```

```python
import itertools

import jax
import jax.numpy as jnp
from jax import lax
from jax.experimental import pallas as pl
from jax.experimental.pallas import tpu as pltpu
from jax.sharding import PartitionSpec as P

BF = jnp.bfloat16
F32 = jnp.float32
MESH = pl.DeviceIdType.MESH
SLOTS = 320
TS = 128
ROWS = 512
FEAT = 128
HID = 256
N_COPIES = 80
CHUNKS = 10
NODES = 131072


def kernel(
    rows_s,
    cols_s,
    count_s,
    feat_hbm,
    deg_ref,
    tiles_hbm,
    weight_ref,
    bias_ref,
    up_hbm,
    hidden_ref,
    fgrad_ref,
    wgrad_ref,
    bgrad_ref,
    feat_v,
    up_v,
    tile_v,
    tile_t,
    sums,
    xblk,
    xtransit,
    mate_out,
    mate_in,
    comb_out,
    comb_in,
    gblk,
    col_out,
    col_mid,
    col_in,
    xsum,
    xsum_transit,
    xsum_in,
    w_send,
    w_y,
    w_z,
    w_zin,
    w_x,
    w_xall,
    w_zall,
    w_all,
    table_v,
    table_s,
    local_sem,
    tile_sem,
    send_sem,
    recv_sem,
):
    rep = lax.axis_index("rep")
    blk = lax.axis_index("blk")
    y = lax.div(rep, 2)
    xh = lax.rem(rep, 2)
    z = lax.div(blk, 4)
    xl = lax.rem(lax.div(blk, 2), 2)
    core = lax.rem(blk, 2)
    y_plus = (lax.rem(rep + 2, 8), blk)
    y_minus = (lax.rem(rep + 6, 8), blk)
    blk_x = blk + 2 - 4 * xl
    x_plus = (2 * y + lax.rem(xh + xl, 2), blk_x)
    x_minus = (2 * y + lax.rem(xh + 1 - xl, 2), blk_x)
    mate = (rep, blk + 1 - 2 * core)
    k_plus = (rep, lax.rem(blk + 2, 32))
    k_minus = (rep, lax.rem(blk + 30, 32))
    single = (rep, lax.rem(blk + 29 + 6 * core, 32))
    y_peers = [(lax.rem(rep + 2 * j, 8), blk) for j in range(1, 4)]
    z_peers = [(rep, lax.rem(blk + 4 * j, 32)) for j in range(1, 8)]
    x_peers = [
        (
            2 * y + lax.rem(xh + j // 4, 2),
            4 * z + 2 * lax.rem(xl + (j // 2) % 2, 2) + lax.rem(core + j % 2, 2),
        )
        for j in range(1, 8)
    ]
    x_place = xh * 4 + xl * 2 + core

    ids = itertools.count()
    started = []

    def send(src, dst, device):
        at = next(ids)
        copy = pltpu.make_async_remote_copy(
            src_ref=src,
            dst_ref=dst,
            send_sem=send_sem.at[at],
            recv_sem=recv_sem.at[at],
            device_id=device,
            device_id_type=MESH,
        )
        copy.start()
        started.append(copy)
        return copy

    half_a = pl.ds(0, FEAT // 2)
    half_b = pl.ds(FEAT // 2, FEAT // 2)

    feat_copy = pltpu.make_async_copy(feat_hbm, feat_v, local_sem.at[0])
    feat_copy.start()
    per_chunk = SLOTS // CHUNKS
    tile_copies = [
        pltpu.make_async_copy(
            tiles_hbm.at[pl.ds(i * per_chunk, per_chunk)],
            tile_v.at[pl.ds(i * per_chunk, per_chunk)],
            tile_sem.at[i],
        )
        for i in range(CHUNKS)
    ]
    for copy in tile_copies:
        copy.start()
    up_copy = pltpu.make_async_copy(up_hbm, up_v, local_sem.at[1])
    up_copy.start()

    barrier = pltpu.get_barrier_semaphore()
    peers = y_peers + z_peers + x_peers + [k_plus, k_minus, single]
    for peer in peers:
        pl.semaphore_signal(barrier, inc=1, device_id=peer, device_id_type=MESH)

    norm = 1.0 / jnp.sqrt(deg_ref[...].astype(F32) + 1.0)
    feat_copy.wait()
    features = feat_v[...].astype(F32)
    own_x = (norm * jnp.concatenate([features[i * TS : (i + 1) * TS].T for i in range(4)], axis=1)).astype(BF)
    xblk[0] = own_x
    pl.semaphore_wait(barrier, len(peers))

    x_a = send(xblk.at[0, half_a], xtransit.at[0], x_plus)
    x_b = send(xblk.at[0, half_b], xtransit.at[1], x_minus)
    own_pa = send(xblk.at[0, half_a], xblk.at[3, half_a], y_plus)
    own_mb = send(xblk.at[0, half_b], xblk.at[1, half_b], y_minus)
    own_pb = send(xblk.at[0, half_b], xblk.at[3, half_b], y_plus)
    own_ma = send(xblk.at[0, half_a], xblk.at[1, half_a], y_minus)

    count = count_s[0]
    places = (
        lax.broadcasted_iota(jnp.int32, (8, 128), 0) * 128
        + lax.broadcasted_iota(jnp.int32, (8, 128), 1)
    )

    def add_slots(i, table):
        for u in range(8):
            t = i * 8 + u
            h = rows_s[t]
            gap = lax.rem(lax.div(h, 4) - blk + 35, 32)
            key = gap * 128 + lax.rem(h, 4) * 32 + cols_s[t]
            key = jnp.where(t < count, key, 4096)
            table = jnp.where(places == key, t, table)
        return table

    table_v[...] = lax.fori_loop(0, SLOTS // 8, add_slots, jnp.full((8, 128), SLOTS, jnp.int32))
    table_copy = pltpu.make_async_copy(table_v, table_s, local_sem.at[2])
    table_copy.start()
    tile_v[SLOTS] = jnp.zeros((TS, TS), BF)
    tile_t[SLOTS] = jnp.zeros((TS, TS), BF)

    x_a.wait_recv()
    fwd_a = send(xtransit.at[0], xblk.at[4, half_a], x_plus)
    x_b.wait_recv()
    fwd_b = send(xtransit.at[1], xblk.at[4, half_b], x_minus)
    own_pa.wait_recv()
    two_a = send(xblk.at[3, half_a], xblk.at[2, half_a], y_plus)
    own_mb.wait_recv()
    two_b = send(xblk.at[1, half_b], xblk.at[2, half_b], y_minus)

    def transpose_chunk(chunk):
        tile_copies[chunk].wait()

        def some(i, carry):
            for u in range(16):
                t = chunk * per_chunk + i * 16 + u
                tile_t[t] = tile_v[t].T
            return carry

        lax.fori_loop(0, per_chunk // 16, some, 0)

    for chunk in range(CHUNKS // 2):
        transpose_chunk(chunk)
    fwd_a.wait_recv()
    far_pa = send(xblk.at[4, half_a], xblk.at[7, half_a], y_plus)
    far_ma = send(xblk.at[4, half_a], xblk.at[5, half_a], y_minus)
    fwd_b.wait_recv()
    far_mb = send(xblk.at[4, half_b], xblk.at[5, half_b], y_minus)
    far_pb = send(xblk.at[4, half_b], xblk.at[7, half_b], y_plus)
    for chunk in range(CHUNKS // 2, CHUNKS):
        transpose_chunk(chunk)
    table_copy.wait()

    def source_block(slot):
        return lax.rem(y + slot % 4, 4) * 2 + lax.rem(xh + slot // 4, 2)

    def value_product(group, slots):
        lhs = jnp.concatenate([xblk[s] for s in slots], axis=1)
        rhs = jnp.concatenate(
            [
                jnp.concatenate(
                    [tile_t[table_s[group, a * 32 + source_block(s) * 4 + b]] for a in range(4)],
                    axis=1,
                )
                for s in slots
                for b in range(4)
            ],
            axis=0,
        )
        return jnp.dot(lhs, rhs, preferred_element_type=F32)

    own_pb.wait_recv()
    own_ma.wait_recv()
    for group in range(7):
        sums[group] = value_product(group, (0, 1, 3))
    far_pa.wait_recv()
    far2_a = send(xblk.at[7, half_a], xblk.at[6, half_a], y_plus)
    far_mb.wait_recv()
    far2_b = send(xblk.at[5, half_b], xblk.at[6, half_b], y_minus)
    two_a.wait_recv()
    two_b.wait_recv()
    for group in range(7):
        sums[group] = sums[group] + value_product(group, (2, 4))
    far_pb.wait_recv()
    far_ma.wait_recv()
    far2_a.wait_recv()
    far2_b.wait_recv()

    def last_value(offset):
        group = offset + 3
        return sums[group] + value_product(group, (5, 7, 6))

    mate_copies = []
    for i, offset in enumerate((-1 - 2 * core, 3 - 2 * core)):
        mate_out[i] = last_value(offset).astype(BF)
        mate_copies.append(send(mate_out.at[i], mate_in.at[i], mate))
    comb_out[2] = last_value(-3 + 6 * core).astype(BF)
    single_copy = send(comb_out.at[2], comb_in.at[2], single)
    minus_part = last_value(-2)
    mate_copies[0].wait_recv()
    comb_out[0] = (minus_part + mate_in[0].astype(F32)).astype(BF)
    minus_copy = send(comb_out.at[0], comb_in.at[0], k_minus)
    plus_part = last_value(2)
    mate_copies[1].wait_recv()
    comb_out[1] = (plus_part + mate_in[1].astype(F32)).astype(BF)
    plus_copy = send(comb_out.at[1], comb_in.at[1], k_plus)
    mate_out[2] = last_value(1 - 2 * core).astype(BF)
    mate_copies.append(send(mate_out.at[2], mate_in.at[2], mate))
    sums[3] = last_value(0) + xblk[0].astype(F32)

    up_copy.wait()
    mate_copies[2].wait_recv()
    total = sums[3] + mate_in[2].astype(F32)
    single_copy.wait_recv()
    total = total + comb_in[2].astype(F32)
    minus_copy.wait_recv()
    plus_copy.wait_recv()
    total = total + comb_in[0].astype(F32) + comb_in[1].astype(F32)
    aggregated = (norm * total).astype(BF)
    weight = weight_ref[...]
    pre_act = (
        lax.dot_general(aggregated, weight, (((0,), (0,)), ((), ())), preferred_element_type=F32)
        + bias_ref[...]
    )
    gate = 1.0 / (1.0 + jnp.exp(-pre_act))
    pre_grad = (
        up_v[...].astype(F32) * (gate + pre_act * gate * (1.0 - gate))
    ).astype(BF)
    gblk[3] = (
        norm * lax.dot_general(weight, pre_grad, (((1,), (1,)), ((), ())), preferred_element_type=F32)
    ).astype(BF)
    g_plus = send(gblk.at[3], gblk.at[1], k_plus)
    g_minus = send(gblk.at[3], gblk.at[5], k_minus)
    g_mate = send(gblk.at[3], gblk.at[2 + 2 * core], mate)
    g_single = send(gblk.at[3], gblk.at[6 - 6 * core], single)
    hidden_ref[...] = (pre_act * gate).astype(BF)

    local_weight = jnp.dot(aggregated, pre_grad, preferred_element_type=F32)
    local_bias = jnp.sum(pre_grad.astype(F32), axis=0, keepdims=True)
    for i in range(4):
        for u in range(8):
            row = i * 32 + (u // 2) * 8
            lanes = slice((u % 2) * 128, (u % 2) * 128 + 128)
            w_send[i, u, 0:8] = local_weight[row : row + 8, lanes]
            w_send[i, u, 8:16] = jnp.broadcast_to(local_bias[:, lanes], (8, 128))
    w_y_copies = [
        send(w_send.at[lax.rem(y + j, 4)], w_y.at[j - 1], y_peers[j - 1]) for j in range(1, 4)
    ]

    def grad_product(source, groups):
        lhs = jnp.concatenate([gblk[g] for g in groups], axis=1)
        rhs = jnp.concatenate(
            [
                jnp.concatenate(
                    [tile_v[table_s[g, a * 32 + source * 4 + b]] for b in range(4)], axis=1
                )
                for g in groups
                for a in range(4)
            ],
            axis=0,
        )
        return jnp.dot(lhs, rhs, preferred_element_type=F32)

    g_mate.wait_recv()
    for slot in range(8):
        sums[slot] = grad_product(source_block(slot), (3, 4 - 2 * core))
    g_plus.wait_recv()
    pass_plus = send(gblk.at[1], gblk.at[2 * core], mate)
    g_minus.wait_recv()
    pass_minus = send(gblk.at[5], gblk.at[4 + 2 * core], mate)
    for slot in range(8):
        sums[slot] = sums[slot] + grad_product(source_block(slot), (1, 5))
    for copy in w_y_copies:
        copy.wait_recv()
    w_z[...] = w_send[y] + w_y[0] + w_y[1] + w_y[2]
    w_z_copies = [
        send(w_z.at[lax.rem(z + j, 8)], w_zin.at[j - 1], z_peers[j - 1]) for j in range(1, 8)
    ]
    g_single.wait_recv()
    pass_plus.wait_recv()
    pass_minus.wait_recv()

    def last_grad(slot):
        rest = (2 - 2 * core, 6 - 2 * core, 6 * core)
        return sums[slot] + grad_product(source_block(slot), rest)

    def first_hop(part):
        col_out[part, 2] = last_grad(part * 4 + 2).astype(BF)
        to_plus = send(col_out.at[part, 2, half_a], col_mid.at[part, 0], y_plus)
        to_minus = send(col_out.at[part, 2, half_b], col_mid.at[part, 1], y_minus)
        return to_plus, to_minus

    def direct_hop(part):
        plus_value = last_grad(part * 4 + 1)
        col_out[part, 1, FEAT // 2 :] = plus_value[FEAT // 2 :].astype(BF)
        plus_b = send(col_out.at[part, 1, half_b], col_in.at[part, 0, half_b], y_plus)
        minus_value = last_grad(part * 4 + 3)
        col_out[part, 3, : FEAT // 2] = minus_value[: FEAT // 2].astype(BF)
        minus_a = send(col_out.at[part, 3, half_a], col_in.at[part, 1, half_a], y_minus)
        sums[part * 4 + 1, : FEAT // 2] = plus_value[: FEAT // 2]
        sums[part * 4 + 3, FEAT // 2 :] = minus_value[FEAT // 2 :]
        return plus_b, minus_a

    def relay_hop(part, to_plus, to_minus):
        to_plus.wait_recv()
        col_out[part, 1, : FEAT // 2] = (
            sums[part * 4 + 1, : FEAT // 2] + col_mid[part, 0].astype(F32)
        ).astype(BF)
        plus_a = send(col_out.at[part, 1, half_a], col_in.at[part, 0, half_a], y_plus)
        to_minus.wait_recv()
        col_out[part, 3, FEAT // 2 :] = (
            sums[part * 4 + 3, FEAT // 2 :] + col_mid[part, 1].astype(F32)
        ).astype(BF)
        minus_b = send(col_out.at[part, 3, half_b], col_in.at[part, 1, half_b], y_minus)
        return plus_a, minus_b

    far_first = first_hop(1)
    far_direct = direct_hop(1)
    far_relay = relay_hop(1, *far_first)
    near_first = first_hop(0)
    sums[4] = last_grad(4)
    near_direct = direct_hop(0)
    near_relay = relay_hop(0, *near_first)
    sums[0] = last_grad(0) + gblk[3].astype(F32)

    for copy in w_z_copies:
        copy.wait_recv()
    w_sum = w_z[z]
    for j in range(7):
        w_sum = w_sum + w_zin[j]
    w_x[...] = w_sum
    w_xall[x_place] = w_sum
    w_x_copies = [send(w_x, w_xall.at[x_place], x_peers[j - 1]) for j in range(1, 8)]

    for copy in far_direct + far_relay:
        copy.wait_recv()
    xsum[...] = (sums[4] + col_in[1, 0].astype(F32) + col_in[1, 1].astype(F32)).astype(BF)
    xs_a = send(xsum.at[half_a], xsum_transit.at[0], x_plus)
    xs_b = send(xsum.at[half_b], xsum_transit.at[1], x_minus)

    for copy in w_x_copies:
        copy.wait_recv()
    w_sum = w_xall[0]
    for j in range(1, 8):
        w_sum = w_sum + w_xall[j]
    w_x_total = w_sum
    w_zall[z] = w_x_total
    w_zin_out = w_all.at[4, 0]
    w_all[4, 0] = w_x_total
    w_g_copies = [send(w_zin_out, w_zall.at[z], z_peers[j - 1]) for j in range(1, 8)]

    xs_a.wait_recv()
    xt_a = send(xsum_transit.at[0], xsum_in.at[half_a], x_plus)
    xs_b.wait_recv()
    xt_b = send(xsum_transit.at[1], xsum_in.at[half_b], x_minus)
    for copy in near_direct + near_relay:
        copy.wait_recv()
    column = sums[0] + col_in[0, 0].astype(F32) + col_in[0, 1].astype(F32)
    for copy in w_g_copies:
        copy.wait_recv()
    w_all[y] = w_zall[...]
    w_f_copies = [send(w_zall, w_all.at[y], y_peers[j - 1]) for j in range(1, 4)]
    xt_a.wait_recv()
    xt_b.wait_recv()
    feature_grad = norm * (column + xsum_in[...].astype(F32))
    for i in range(4):
        fgrad_ref[i * TS : (i + 1) * TS, :] = feature_grad[:, i * TS : (i + 1) * TS].T.astype(BF)
    scale = NODES ** (-0.5)
    for copy in w_f_copies:
        copy.wait_recv()
    bgrad_ref[:, 0:128] = w_all[0, 0, 8:9] * scale
    bgrad_ref[:, 128:256] = w_all[0, 1, 8:9] * scale
    for i in range(4):
        for u in range(8):
            row = i * 32 + (u // 2) * 8
            lane = (u % 2) * 128
            wgrad_ref[row : row + 8, lane : lane + 128] = w_all[i, u, 0:8] * scale
    for copy in started:
        copy.wait_send()


def on_device(
    features, degrees, tile_weights, tile_rows, tile_cols, tile_counts, weight, layer_bias, upstream
):
    vmem = pl.BlockSpec(memory_space=pltpu.VMEM)
    smem = pl.BlockSpec(memory_space=pltpu.SMEM)
    anywhere = pl.BlockSpec(memory_space=pl.ANY)
    blocks = lambda *lead: pltpu.VMEM((*lead, FEAT, ROWS), BF)
    halves = lambda *lead: pltpu.VMEM((*lead, FEAT // 2, ROWS), BF)
    units = lambda *lead: pltpu.VMEM((*lead, 16, 128), F32)
    hidden, feature_grad, weight_grad, bias_grad = pl.pallas_call(
        kernel,
        in_specs=[smem, smem, smem, anywhere, vmem, anywhere, vmem, vmem, anywhere],
        out_specs=[vmem, vmem, vmem, vmem],
        out_shape=[
            jax.ShapeDtypeStruct((ROWS, HID), BF),
            jax.ShapeDtypeStruct((ROWS, FEAT), BF),
            jax.ShapeDtypeStruct((FEAT, HID), F32),
            jax.ShapeDtypeStruct((1, HID), F32),
        ],
        scratch_shapes=[
            pltpu.VMEM((ROWS, FEAT), BF),
            pltpu.VMEM((ROWS, HID), BF),
            pltpu.VMEM((SLOTS + 1, TS, TS), BF),
            pltpu.VMEM((SLOTS + 1, TS, TS), BF),
            pltpu.VMEM((8, FEAT, ROWS), F32),
            blocks(8),
            halves(2),
            blocks(3),
            blocks(3),
            blocks(3),
            blocks(3),
            blocks(7),
            blocks(2, 4),
            halves(2, 2),
            blocks(2, 2),
            blocks(),
            halves(2),
            blocks(),
            units(4, 8),
            units(3, 8),
            units(8),
            units(7),
            units(),
            units(8),
            units(8),
            units(5, 8),
            pltpu.VMEM((8, 128), jnp.int32),
            pltpu.SMEM((8, 128), jnp.int32),
            pltpu.SemaphoreType.DMA((3,)),
            pltpu.SemaphoreType.DMA((CHUNKS,)),
            pltpu.SemaphoreType.DMA((N_COPIES,)),
            pltpu.SemaphoreType.DMA((N_COPIES,)),
        ],
        compiler_params=pltpu.CompilerParams(
            collective_id=0, has_side_effects=True, vmem_limit_bytes=56 << 20
        ),
        name="layer",
    )(
        tile_rows.reshape(SLOTS),
        tile_cols.reshape(SLOTS),
        tile_counts.reshape(1),
        features,
        degrees.reshape(1, ROWS),
        tile_weights.reshape(SLOTS, TS, TS),
        weight,
        layer_bias.reshape(1, HID),
        upstream,
    )
    return hidden, feature_grad, weight_grad, bias_grad.reshape(HID)


def solution(mesh):
    placed = (
        P(("rep", "blk"), None),
        P(("rep", "blk")),
        P("rep", "blk", None, None, None),
        P("rep", "blk", None),
        P("rep", "blk", None),
        P("rep", "blk"),
        P(),
        P(),
        P(("rep", "blk"), None),
    )
    return jax.shard_map(
        on_device,
        mesh=mesh,
        in_specs=placed,
        out_specs=(P(("rep", "blk"), None), P(("rep", "blk"), None), P(), P()),
        check_vma=False,
    )
```

```python
import itertools

import jax
import jax.numpy as jnp
from jax import lax
from jax.experimental import pallas as pl
from jax.experimental.pallas import tpu as pltpu
from jax.sharding import PartitionSpec as P

BF = jnp.bfloat16
F32 = jnp.float32
MESH = pl.DeviceIdType.MESH
SLOTS = 320
TS = 128
ROWS = 512
FEAT = 128
HID = 256
QUARTER = 32
N_COPIES = 128
CHUNKS = 10
NODES = 131072


def kernel(
    rows_s,
    cols_s,
    count_hbm,
    feat_hbm,
    deg_ref,
    tiles_hbm,
    weight_ref,
    bias_ref,
    up_hbm,
    hidden_ref,
    fgrad_ref,
    wgrad_ref,
    bgrad_ref,
    feat_v,
    up_v,
    tile_v,
    tile_t,
    sums,
    xblk,
    xtransit,
    mate_out,
    mate_in,
    comb_out,
    comb_in,
    gblk,
    col_out,
    col_mid,
    col_in,
    xsum,
    xsum_transit,
    xsum_in,
    w_send,
    w_y,
    w_z,
    w_zin,
    w_x,
    w_xall,
    w_x_total,
    w_zall,
    w_all,
    table_v,
    table_s,
    count_s,
    local_sem,
    tile_sem,
    send_sem,
    recv_sem,
):
    rep = lax.axis_index("rep")
    blk = lax.axis_index("blk")
    y = lax.div(rep, 2)
    xh = lax.rem(rep, 2)
    z = lax.div(blk, 4)
    xl = lax.rem(lax.div(blk, 2), 2)
    core = lax.rem(blk, 2)
    y_plus = (lax.rem(rep + 2, 8), blk)
    y_minus = (lax.rem(rep + 6, 8), blk)
    blk_x = blk + 2 - 4 * xl
    x_plus = (2 * y + lax.rem(xh + xl, 2), blk_x)
    x_minus = (2 * y + lax.rem(xh + 1 - xl, 2), blk_x)
    mate = (rep, blk + 1 - 2 * core)
    k_plus = (rep, lax.rem(blk + 2, 32))
    k_minus = (rep, lax.rem(blk + 30, 32))
    single = (rep, lax.rem(blk + 29 + 6 * core, 32))
    y_peers = [(lax.rem(rep + 2 * j, 8), blk) for j in range(1, 4)]
    z_peers = [(rep, lax.rem(blk + 4 * j, 32)) for j in range(1, 8)]
    x_peers = [
        (
            2 * y + lax.rem(xh + j // 4, 2),
            4 * z + 2 * lax.rem(xl + (j // 2) % 2, 2) + lax.rem(core + j % 2, 2),
        )
        for j in range(1, 8)
    ]
    x_place = xh * 4 + xl * 2 + core

    ids = itertools.count()
    started = []

    def send(src, dst, device):
        at = next(ids)
        copy = pltpu.make_async_remote_copy(
            src_ref=src,
            dst_ref=dst,
            send_sem=send_sem.at[at],
            recv_sem=recv_sem.at[at],
            device_id=device,
            device_id_type=MESH,
        )
        copy.start()
        started.append(copy)
        return copy

    low = [pl.ds(i * QUARTER, QUARTER) for i in range(2)]
    high = [pl.ds(FEAT // 2 + i * QUARTER, QUARTER) for i in range(2)]

    def send_parts(src, dst, parts, device):
        return [send(src.at[part], dst.at[part], device) for part in parts]

    def arrived(copies):
        for copy in copies:
            copy.wait_recv()

    feat_copy = pltpu.make_async_copy(feat_hbm, feat_v, local_sem.at[0])
    feat_copy.start()
    count_copy = pltpu.make_async_copy(count_hbm, count_s, local_sem.at[3])
    count_copy.start()
    per_chunk = SLOTS // CHUNKS
    tile_copies = [
        pltpu.make_async_copy(
            tiles_hbm.at[pl.ds(i * per_chunk, per_chunk)],
            tile_v.at[pl.ds(i * per_chunk, per_chunk)],
            tile_sem.at[i],
        )
        for i in range(CHUNKS)
    ]
    for copy in tile_copies:
        copy.start()
    up_copy = pltpu.make_async_copy(up_hbm, up_v, local_sem.at[1])
    up_copy.start()

    barrier = pltpu.get_barrier_semaphore()
    peers = y_peers + z_peers + x_peers + [k_plus, k_minus, single]
    for peer in peers:
        pl.semaphore_signal(barrier, inc=1, device_id=peer, device_id_type=MESH)

    norm = 1.0 / jnp.sqrt(deg_ref[...].astype(F32) + 1.0)
    feat_copy.wait()
    features = feat_v[...].astype(F32)
    own_x = (norm * jnp.concatenate([features[i * TS : (i + 1) * TS].T for i in range(4)], axis=1)).astype(BF)
    xblk[0] = own_x
    pl.semaphore_wait(barrier, len(peers))

    own = xblk.at[0]
    x_a = [send(own.at[low[i]], xtransit.at[0, i], x_plus) for i in range(2)]
    x_b = [send(own.at[high[i]], xtransit.at[1, i], x_minus) for i in range(2)]
    own_pa, own_mb, own_pb, own_ma = [], [], [], []
    for i in range(2):
        own_pa.append(send(own.at[low[i]], xblk.at[3, low[i]], y_plus))
        own_mb.append(send(own.at[high[i]], xblk.at[1, high[i]], y_minus))
    for i in range(2):
        own_pb.append(send(own.at[high[i]], xblk.at[3, high[i]], y_plus))
        own_ma.append(send(own.at[low[i]], xblk.at[1, low[i]], y_minus))

    count_copy.wait()
    count = count_s[0, 0]
    places = (
        lax.broadcasted_iota(jnp.int32, (8, 128), 0) * 128
        + lax.broadcasted_iota(jnp.int32, (8, 128), 1)
    )

    def add_slots(i, table):
        for u in range(8):
            t = i * 8 + u
            h = rows_s[0, 0, t]
            gap = lax.rem(lax.div(h, 4) - blk + 35, 32)
            key = gap * 128 + lax.rem(h, 4) * 32 + cols_s[0, 0, t]
            key = jnp.where(t < count, key, 4096)
            table = jnp.where(places == key, t, table)
        return table

    table_v[...] = lax.fori_loop(0, SLOTS // 8, add_slots, jnp.full((8, 128), SLOTS, jnp.int32))
    table_copy = pltpu.make_async_copy(table_v, table_s, local_sem.at[2])
    table_copy.start()
    tile_v[SLOTS] = jnp.zeros((TS, TS), BF)
    tile_t[SLOTS] = jnp.zeros((TS, TS), BF)

    fwd_a, fwd_b, two_a, two_b = [], [], [], []
    for i in range(2):
        x_a[i].wait_recv()
        fwd_a.append(send(xtransit.at[0, i], xblk.at[4, low[i]], x_plus))
        x_b[i].wait_recv()
        fwd_b.append(send(xtransit.at[1, i], xblk.at[4, high[i]], x_minus))
        own_pa[i].wait_recv()
        two_a.append(send(xblk.at[3, low[i]], xblk.at[2, low[i]], y_plus))
        own_mb[i].wait_recv()
        two_b.append(send(xblk.at[1, high[i]], xblk.at[2, high[i]], y_minus))

    def transpose_chunk(chunk):
        tile_copies[chunk].wait()

        def some(i, carry):
            for u in range(16):
                t = chunk * per_chunk + i * 16 + u
                tile_t[t] = tile_v[t].T
            return carry

        lax.fori_loop(0, per_chunk // 16, some, 0)

    for chunk in range(4):
        transpose_chunk(chunk)
    far_pa, far_ma, far_pb, far_mb = [], [], [], []
    for i in range(2):
        fwd_a[i].wait_recv()
        far_pa.append(send(xblk.at[4, low[i]], xblk.at[7, low[i]], y_plus))
        fwd_b[i].wait_recv()
        far_mb.append(send(xblk.at[4, high[i]], xblk.at[5, high[i]], y_minus))
        far_ma.append(send(xblk.at[4, low[i]], xblk.at[5, low[i]], y_minus))
        far_pb.append(send(xblk.at[4, high[i]], xblk.at[7, high[i]], y_plus))
    for chunk in range(4, CHUNKS):
        transpose_chunk(chunk)
    far2_a, far2_b = [], []
    for i in range(2):
        far_pa[i].wait_recv()
        far2_a.append(send(xblk.at[7, low[i]], xblk.at[6, low[i]], y_plus))
        far_mb[i].wait_recv()
        far2_b.append(send(xblk.at[5, high[i]], xblk.at[6, high[i]], y_minus))
    table_copy.wait()

    def source_block(slot):
        return lax.rem(y + slot % 4, 4) * 2 + lax.rem(xh + slot // 4, 2)

    def value_product(group, slots):
        lhs = jnp.concatenate([xblk[s] for s in slots], axis=1)
        rhs = jnp.concatenate(
            [
                jnp.concatenate(
                    [tile_t[table_s[group, a * 32 + source_block(s) * 4 + b]] for a in range(4)],
                    axis=1,
                )
                for s in slots
                for b in range(4)
            ],
            axis=0,
        )
        return jnp.dot(lhs, rhs, preferred_element_type=F32)

    arrived(own_pb + own_ma)
    for group in range(7):
        sums[group] = value_product(group, (0, 1, 3))
    arrived(two_a + two_b + far_pb + far_ma)
    for group in range(7):
        sums[group] = sums[group] + value_product(group, (2, 4, 5, 7))
    arrived(far2_a + far2_b)

    def last_value(offset):
        group = offset + 3
        return sums[group] + value_product(group, (6,))

    mate_copies = []
    for i, offset in enumerate((-1 - 2 * core, 3 - 2 * core)):
        mate_out[i] = last_value(offset).astype(BF)
        mate_copies.append(send(mate_out.at[i], mate_in.at[i], mate))
    comb_out[2] = last_value(-3 + 6 * core).astype(BF)
    single_copy = send(comb_out.at[2], comb_in.at[2], single)
    minus_part = last_value(-2)
    mate_copies[0].wait_recv()
    comb_out[0] = (minus_part + mate_in[0].astype(F32)).astype(BF)
    minus_copy = send(comb_out.at[0], comb_in.at[0], k_minus)
    plus_part = last_value(2)
    mate_copies[1].wait_recv()
    comb_out[1] = (plus_part + mate_in[1].astype(F32)).astype(BF)
    plus_copy = send(comb_out.at[1], comb_in.at[1], k_plus)
    mate_out[2] = last_value(1 - 2 * core).astype(BF)
    mate_copies.append(send(mate_out.at[2], mate_in.at[2], mate))
    sums[3] = last_value(0) + xblk[0].astype(F32)

    up_copy.wait()
    mate_copies[2].wait_recv()
    total = sums[3] + mate_in[2].astype(F32)
    single_copy.wait_recv()
    total = total + comb_in[2].astype(F32)
    minus_copy.wait_recv()
    plus_copy.wait_recv()
    total = total + comb_in[0].astype(F32) + comb_in[1].astype(F32)
    aggregated = (norm * total).astype(BF)
    weight = weight_ref[...]
    pre_act = (
        lax.dot_general(aggregated, weight, (((0,), (0,)), ((), ())), preferred_element_type=F32)
        + bias_ref[...]
    )
    gate = 1.0 / (1.0 + jnp.exp(-pre_act))
    pre_grad = (
        up_v[...].astype(F32) * (gate + pre_act * gate * (1.0 - gate))
    ).astype(BF)
    gblk[3] = (
        norm * lax.dot_general(weight, pre_grad, (((1,), (1,)), ((), ())), preferred_element_type=F32)
    ).astype(BF)
    g_plus = send(gblk.at[3], gblk.at[1], k_plus)
    g_minus = send(gblk.at[3], gblk.at[5], k_minus)
    g_mate = send(gblk.at[3], gblk.at[2 + 2 * core], mate)
    g_single = send(gblk.at[3], gblk.at[6 - 6 * core], single)
    hidden_ref[...] = (pre_act * gate).astype(BF)

    local_weight = jnp.dot(aggregated, pre_grad, preferred_element_type=F32)
    local_bias = jnp.sum(pre_grad.astype(F32), axis=0, keepdims=True)
    for i in range(4):
        for u in range(8):
            row = i * 32 + (u // 2) * 8
            lanes = slice((u % 2) * 128, (u % 2) * 128 + 128)
            w_send[i, u, 0:8] = local_weight[row : row + 8, lanes]
            w_send[i, u, 8:16] = jnp.broadcast_to(local_bias[:, lanes], (8, 128))
    w_y_copies = [
        send(w_send.at[lax.rem(y + j, 4)], w_y.at[y], y_peers[j - 1]) for j in range(1, 4)
    ]
    w_y[y] = w_send[y]

    def grad_product(source, groups):
        lhs = jnp.concatenate([gblk[g] for g in groups], axis=1)
        rhs = jnp.concatenate(
            [
                jnp.concatenate(
                    [tile_v[table_s[g, a * 32 + source * 4 + b]] for b in range(4)], axis=1
                )
                for g in groups
                for a in range(4)
            ],
            axis=0,
        )
        return jnp.dot(lhs, rhs, preferred_element_type=F32)

    g_mate.wait_recv()
    for slot in range(8):
        sums[slot] = grad_product(source_block(slot), (3, 4 - 2 * core))
    g_plus.wait_recv()
    pass_plus = send(gblk.at[1], gblk.at[2 * core], mate)
    g_minus.wait_recv()
    pass_minus = send(gblk.at[5], gblk.at[4 + 2 * core], mate)
    arrived(w_y_copies)
    w_z[...] = w_y[0] + w_y[1] + w_y[2] + w_y[3]
    w_z_copies = [
        send(w_z.at[lax.rem(z + j, 8)], w_zin.at[j - 1], z_peers[j - 1]) for j in range(1, 8)
    ]
    for slot in range(8):
        sums[slot] = sums[slot] + grad_product(source_block(slot), (1, 5))
    arrived([g_single, pass_plus, pass_minus])

    def last_grad(slot):
        rest = (2 - 2 * core, 6 - 2 * core, 6 * core)
        return sums[slot] + grad_product(source_block(slot), rest)

    def first_hop(part):
        col_out[part, 2] = last_grad(part * 4 + 2).astype(BF)
        source = col_out.at[part, 2]
        to_plus = [send(source.at[low[i]], col_mid.at[part, 0, i], y_plus) for i in range(2)]
        to_minus = [send(source.at[high[i]], col_mid.at[part, 1, i], y_minus) for i in range(2)]
        return to_plus, to_minus

    def direct_hop(part):
        col_out[part, 1, FEAT // 2 :] = sums[part * 4 + 1, FEAT // 2 :].astype(BF)
        plus_b = send_parts(col_out.at[part, 1], col_in.at[part, 0], high, y_plus)
        col_out[part, 3, : FEAT // 2] = sums[part * 4 + 3, : FEAT // 2].astype(BF)
        minus_a = send_parts(col_out.at[part, 3], col_in.at[part, 1], low, y_minus)
        return plus_b, minus_a

    def relay_hop(part, to_plus, to_minus):
        plus_a, minus_b = [], []
        for i in range(2):
            to_plus[i].wait_recv()
            col_out[part, 1, low[i]] = (
                sums[part * 4 + 1, low[i]] + col_mid[part, 0, i].astype(F32)
            ).astype(BF)
            plus_a.append(
                send(col_out.at[part, 1, low[i]], col_in.at[part, 0, low[i]], y_plus)
            )
            to_minus[i].wait_recv()
            col_out[part, 3, high[i]] = (
                sums[part * 4 + 3, high[i]] + col_mid[part, 1, i].astype(F32)
            ).astype(BF)
            minus_b.append(
                send(col_out.at[part, 3, high[i]], col_in.at[part, 1, high[i]], y_minus)
            )
        return plus_a, minus_b

    far_first = first_hop(1)
    for slot in (5, 7):
        sums[slot] = last_grad(slot)
    far_plus_b, far_minus_a = direct_hop(1)
    for slot in (4, 1, 3):
        sums[slot] = last_grad(slot)
    arrived(w_z_copies)
    w_sum = w_z[z]
    for j in range(7):
        w_sum = w_sum + w_zin[j]
    w_x[...] = w_sum
    w_xall[x_place] = w_sum
    w_x_copies = [send(w_x, w_xall.at[x_place], x_peers[j - 1]) for j in range(1, 8)]
    far_plus_a, far_minus_b = relay_hop(1, *far_first)
    near_first = first_hop(0)
    near_plus_b, near_minus_a = direct_hop(0)
    sums[0] = last_grad(0) + gblk[3].astype(F32)

    arrived(w_x_copies)
    w_sum = w_xall[0]
    for j in range(1, 8):
        w_sum = w_sum + w_xall[j]
    w_x_total[...] = w_sum
    w_zall[z] = w_sum
    w_g_copies = [send(w_x_total, w_zall.at[z], z_peers[j - 1]) for j in range(1, 8)]

    def partner_sum(part):
        xsum[part] = (
            sums[4, part] + col_in[1, 0, part].astype(F32) + col_in[1, 1, part].astype(F32)
        ).astype(BF)

    arrived(far_plus_b + far_minus_a)
    xs_a, xs_b = [], []
    for i in range(2):
        far_plus_a[i].wait_recv()
        partner_sum(low[i])
        xs_a.append(send(xsum.at[low[i]], xsum_transit.at[0, i], x_plus))
        far_minus_b[i].wait_recv()
        partner_sum(high[i])
        xs_b.append(send(xsum.at[high[i]], xsum_transit.at[1, i], x_minus))
    near_plus_a, near_minus_b = relay_hop(0, *near_first)
    xt_a, xt_b = [], []
    for i in range(2):
        xs_a[i].wait_recv()
        xt_a.append(send(xsum_transit.at[0, i], xsum_in.at[low[i]], x_plus))
        xs_b[i].wait_recv()
        xt_b.append(send(xsum_transit.at[1, i], xsum_in.at[high[i]], x_minus))
    arrived(w_g_copies)
    w_f_copies = [
        send(w_zall.at[:, pl.ds(0, 8)], w_all.at[y], y_peers[j - 1]) for j in range(1, 4)
    ]
    w_all[y] = w_zall[:, 0:8]
    scale = NODES ** (-0.5)
    bgrad_ref[:, 0:128] = w_zall[0, 8:9] * scale
    bgrad_ref[:, 128:256] = w_zall[1, 8:9] * scale
    arrived(near_plus_b + near_minus_a + near_plus_a + near_minus_b)
    column = sums[0] + col_in[0, 0].astype(F32) + col_in[0, 1].astype(F32)
    arrived(w_f_copies)
    for i in range(4):
        for u in range(8):
            row = i * 32 + (u // 2) * 8
            lane = (u % 2) * 128
            wgrad_ref[row : row + 8, lane : lane + 128] = w_all[i, u] * scale
    arrived(xt_a + xt_b)
    feature_grad = norm * (column + xsum_in[...].astype(F32))
    for i in range(4):
        fgrad_ref[i * TS : (i + 1) * TS, :] = feature_grad[:, i * TS : (i + 1) * TS].T.astype(BF)
    for copy in started:
        copy.wait_send()


def settle(*refs):
    for source, target in zip(refs[:4], refs[4:]):
        target[...] = source[...]


def on_device(
    features, degrees, tile_weights, tile_rows, tile_cols, tile_counts, weight, layer_bias, upstream
):
    vmem = pl.BlockSpec(memory_space=pltpu.VMEM)
    smem = pl.BlockSpec(memory_space=pltpu.SMEM)
    anywhere = pl.BlockSpec(memory_space=pl.ANY)
    blocks = lambda *lead: pltpu.VMEM((*lead, FEAT, ROWS), BF)
    quarters = lambda *lead: pltpu.VMEM((*lead, QUARTER, ROWS), BF)
    units = lambda *lead: pltpu.VMEM((*lead, 16, 128), F32)
    shapes = [
        jax.ShapeDtypeStruct((ROWS, HID), BF),
        jax.ShapeDtypeStruct((ROWS, FEAT), BF),
        jax.ShapeDtypeStruct((FEAT, HID), F32),
        jax.ShapeDtypeStruct((1, HID), F32),
    ]
    results = pl.pallas_call(
        kernel,
        in_specs=[smem, smem, anywhere, anywhere, vmem, anywhere, vmem, vmem, anywhere],
        out_specs=[vmem, vmem, vmem, vmem],
        out_shape=shapes,
        scratch_shapes=[
            pltpu.VMEM((ROWS, FEAT), BF),
            pltpu.VMEM((ROWS, HID), BF),
            pltpu.VMEM((SLOTS + 1, TS, TS), BF),
            pltpu.VMEM((SLOTS + 1, TS, TS), BF),
            pltpu.VMEM((8, FEAT, ROWS), F32),
            blocks(8),
            quarters(2, 2),
            blocks(3),
            blocks(3),
            blocks(3),
            blocks(3),
            blocks(7),
            blocks(2, 4),
            quarters(2, 2, 2),
            blocks(2, 2),
            blocks(),
            quarters(2, 2),
            blocks(),
            units(4, 8),
            units(4, 8),
            units(8),
            units(7),
            units(),
            units(8),
            units(),
            units(8),
            pltpu.VMEM((4, 8, 8, 128), F32),
            pltpu.VMEM((8, 128), jnp.int32),
            pltpu.SMEM((8, 128), jnp.int32),
            pltpu.SMEM((1, 1), jnp.int32),
            pltpu.SemaphoreType.DMA((4,)),
            pltpu.SemaphoreType.DMA((CHUNKS,)),
            pltpu.SemaphoreType.DMA((N_COPIES,)),
            pltpu.SemaphoreType.DMA((N_COPIES,)),
        ],
        compiler_params=pltpu.CompilerParams(
            collective_id=0, has_side_effects=True, vmem_limit_bytes=56 << 20
        ),
        name="layer",
    )(
        tile_rows,
        tile_cols,
        tile_counts,
        features,
        degrees.reshape(1, ROWS),
        tile_weights.reshape(SLOTS, TS, TS),
        weight,
        layer_bias.reshape(1, HID),
        upstream,
    )
    hidden, feature_grad, weight_grad, bias_grad = pl.pallas_call(
        settle, in_specs=[vmem] * 4, out_specs=[vmem] * 4, out_shape=shapes, name="settle"
    )(*results)
    return hidden, feature_grad, weight_grad, bias_grad.reshape(HID)


def solution(mesh):
    placed = (
        P(("rep", "blk"), None),
        P(("rep", "blk")),
        P("rep", "blk", None, None, None),
        P("rep", "blk", None),
        P("rep", "blk", None),
        P("rep", "blk"),
        P(),
        P(),
        P(("rep", "blk"), None),
    )
    return jax.shard_map(
        on_device,
        mesh=mesh,
        in_specs=placed,
        out_specs=(P(("rep", "blk"), None), P(("rep", "blk"), None), P(), P()),
        check_vma=False,
    )
```

```python
import itertools

import jax
import jax.numpy as jnp
from jax import lax
from jax.experimental import pallas as pl
from jax.experimental.pallas import tpu as pltpu
from jax.sharding import PartitionSpec as P

BF = jnp.bfloat16
F32 = jnp.float32
MESH = pl.DeviceIdType.MESH
SLOTS = 320
TS = 128
ROWS = 512
HALF = 256
FEAT = 128
HID = 256
QUARTER = 32
N_COPIES = 128
CHUNKS = 10
NODES = 131072


def kernel(
    rows_s,
    cols_s,
    count_hbm,
    feat_hbm,
    deg_ref,
    tiles_hbm,
    weight_ref,
    bias_ref,
    up_hbm,
    hidden_ref,
    fgrad_ref,
    wgrad_ref,
    bgrad_ref,
    feat_v,
    up_v,
    tile_v,
    tile_t,
    sums,
    xblk,
    xtransit,
    mate_out,
    mate_in,
    comb_out,
    comb_in,
    gblk,
    col_out,
    col_mid,
    col_in,
    xsum,
    xsum_transit,
    xsum_in,
    w_send,
    w_y,
    w_z,
    w_zin,
    w_x,
    w_xall,
    w_x_total,
    w_zall,
    w_all,
    table_v,
    table_s,
    count_s,
    local_sem,
    tile_sem,
    send_sem,
    recv_sem,
):
    rep = lax.axis_index("rep")
    blk = lax.axis_index("blk")
    y = lax.div(rep, 2)
    xh = lax.rem(rep, 2)
    z = lax.div(blk, 4)
    xl = lax.rem(lax.div(blk, 2), 2)
    core = lax.rem(blk, 2)
    y_plus = (lax.rem(rep + 2, 8), blk)
    y_minus = (lax.rem(rep + 6, 8), blk)
    blk_x = blk + 2 - 4 * xl
    x_plus = (2 * y + lax.rem(xh + xl, 2), blk_x)
    x_minus = (2 * y + lax.rem(xh + 1 - xl, 2), blk_x)
    mate = (rep, blk + 1 - 2 * core)
    k_plus = (rep, lax.rem(blk + 2, 32))
    k_minus = (rep, lax.rem(blk + 30, 32))
    single = (rep, lax.rem(blk + 29 + 6 * core, 32))
    y_peers = [(lax.rem(rep + 2 * j, 8), blk) for j in range(1, 4)]
    z_peers = [(rep, lax.rem(blk + 4 * j, 32)) for j in range(1, 8)]
    x_peers = [
        (
            2 * y + lax.rem(xh + j // 4, 2),
            4 * z + 2 * lax.rem(xl + (j // 2) % 2, 2) + lax.rem(core + j % 2, 2),
        )
        for j in range(1, 8)
    ]
    x_place = xh * 4 + xl * 2 + core

    ids = itertools.count()
    started = []

    def send(src, dst, device):
        at = next(ids)
        copy = pltpu.make_async_remote_copy(
            src_ref=src,
            dst_ref=dst,
            send_sem=send_sem.at[at],
            recv_sem=recv_sem.at[at],
            device_id=device,
            device_id_type=MESH,
        )
        copy.start()
        started.append(copy)
        return copy

    low = [pl.ds(i * QUARTER, QUARTER) for i in range(2)]
    high = [pl.ds(FEAT // 2 + i * QUARTER, QUARTER) for i in range(2)]

    def send_parts(src, dst, parts, device):
        return [send(src.at[part], dst.at[part], device) for part in parts]

    def arrived(copies):
        for copy in copies:
            copy.wait_recv()

    feat_copy = pltpu.make_async_copy(feat_hbm, feat_v, local_sem.at[0])
    feat_copy.start()
    count_copy = pltpu.make_async_copy(count_hbm, count_s, local_sem.at[3])
    count_copy.start()
    per_chunk = SLOTS // CHUNKS
    tile_copies = [
        pltpu.make_async_copy(
            tiles_hbm.at[pl.ds(i * per_chunk, per_chunk)],
            tile_v.at[pl.ds(i * per_chunk, per_chunk)],
            tile_sem.at[i],
        )
        for i in range(CHUNKS)
    ]
    for copy in tile_copies:
        copy.start()
    up_copy = pltpu.make_async_copy(up_hbm, up_v, local_sem.at[1])
    up_copy.start()

    barrier = pltpu.get_barrier_semaphore()
    peers = y_peers + z_peers + x_peers + [k_plus, k_minus, single]
    for peer in peers:
        pl.semaphore_signal(barrier, inc=1, device_id=peer, device_id_type=MESH)

    norm = 1.0 / jnp.sqrt(deg_ref[...].astype(F32) + 1.0)
    feat_copy.wait()
    features = feat_v[...].astype(F32)
    own_x = (norm * jnp.concatenate([features[i * TS : (i + 1) * TS].T for i in range(4)], axis=1)).astype(BF)
    xblk[0] = own_x
    pl.semaphore_wait(barrier, len(peers))

    own = xblk.at[0]
    x_a = [send(own.at[low[i]], xtransit.at[0, i], x_plus) for i in range(2)]
    x_b = [send(own.at[high[i]], xtransit.at[1, i], x_minus) for i in range(2)]
    own_pa, own_mb, own_pb, own_ma = [], [], [], []
    for i in range(2):
        own_pa.append(send(own.at[low[i]], xblk.at[3, low[i]], y_plus))
        own_mb.append(send(own.at[high[i]], xblk.at[1, high[i]], y_minus))
    for i in range(2):
        own_pb.append(send(own.at[high[i]], xblk.at[3, high[i]], y_plus))
        own_ma.append(send(own.at[low[i]], xblk.at[1, low[i]], y_minus))

    count_copy.wait()
    count = count_s[0, 0]
    places = (
        lax.broadcasted_iota(jnp.int32, (8, 128), 0) * 128
        + lax.broadcasted_iota(jnp.int32, (8, 128), 1)
    )

    def add_slots(i, table):
        for u in range(8):
            t = i * 8 + u
            h = rows_s[0, 0, t]
            gap = lax.rem(lax.div(h, 4) - blk + 35, 32)
            key = gap * 128 + lax.rem(h, 4) * 32 + cols_s[0, 0, t]
            key = jnp.where(t < count, key, 4096)
            table = jnp.where(places == key, t, table)
        return table

    table_v[...] = lax.fori_loop(0, SLOTS // 8, add_slots, jnp.full((8, 128), SLOTS, jnp.int32))
    table_copy = pltpu.make_async_copy(table_v, table_s, local_sem.at[2])
    table_copy.start()
    tile_v[SLOTS] = jnp.zeros((TS, TS), BF)
    tile_t[SLOTS] = jnp.zeros((TS, TS), BF)

    fwd_a, fwd_b, two_a, two_b = [], [], [], []
    for i in range(2):
        x_a[i].wait_recv()
        fwd_a.append(send(xtransit.at[0, i], xblk.at[4, low[i]], x_plus))
        x_b[i].wait_recv()
        fwd_b.append(send(xtransit.at[1, i], xblk.at[4, high[i]], x_minus))
        own_pa[i].wait_recv()
        two_a.append(send(xblk.at[3, low[i]], xblk.at[2, low[i]], y_plus))
        own_mb[i].wait_recv()
        two_b.append(send(xblk.at[1, high[i]], xblk.at[2, high[i]], y_minus))

    def transpose_chunk(chunk):
        tile_copies[chunk].wait()

        def some(i, carry):
            for u in range(16):
                t = chunk * per_chunk + i * 16 + u
                tile_t[t] = tile_v[t].T
            return carry

        lax.fori_loop(0, per_chunk // 16, some, 0)

    for chunk in range(4):
        transpose_chunk(chunk)
    far_pa, far_ma, far_pb, far_mb = [], [], [], []
    for i in range(2):
        fwd_a[i].wait_recv()
        far_pa.append(send(xblk.at[4, low[i]], xblk.at[7, low[i]], y_plus))
        fwd_b[i].wait_recv()
        far_mb.append(send(xblk.at[4, high[i]], xblk.at[5, high[i]], y_minus))
        far_ma.append(send(xblk.at[4, low[i]], xblk.at[5, low[i]], y_minus))
        far_pb.append(send(xblk.at[4, high[i]], xblk.at[7, high[i]], y_plus))
    for chunk in range(4, CHUNKS):
        transpose_chunk(chunk)
    far2_a, far2_b = [], []
    for i in range(2):
        far_pa[i].wait_recv()
        far2_a.append(send(xblk.at[7, low[i]], xblk.at[6, low[i]], y_plus))
        far_mb[i].wait_recv()
        far2_b.append(send(xblk.at[5, high[i]], xblk.at[6, high[i]], y_minus))
    table_copy.wait()

    def source_block(slot):
        return lax.rem(y + slot % 4, 4) * 2 + lax.rem(xh + slot // 4, 2)

    def value_product(group, slots):
        lhs = jnp.concatenate([xblk[s] for s in slots], axis=1)
        rhs = jnp.concatenate(
            [
                jnp.concatenate(
                    [tile_t[table_s[group, a * 32 + source_block(s) * 4 + b]] for a in range(4)],
                    axis=1,
                )
                for s in slots
                for b in range(4)
            ],
            axis=0,
        )
        return jnp.dot(lhs, rhs, preferred_element_type=F32)

    arrived(own_pb + own_ma)
    for group in range(7):
        sums[group] = value_product(group, (0, 1, 3))
    arrived(two_a + two_b)
    for group in range(7):
        sums[group] = sums[group] + value_product(group, (2, 4))
    arrived(far_pb + far_ma)
    for group in range(7):
        sums[group] = sums[group] + value_product(group, (5, 7))
    arrived(far2_a + far2_b)

    def last_value(offset):
        group = offset + 3
        return sums[group] + value_product(group, (6,))

    columns = [slice(h * HALF, (h + 1) * HALF) for h in range(2)]
    mate_copies = [[], [], []]
    for i, offset in enumerate((-1 - 2 * core, 3 - 2 * core)):
        value = last_value(offset).astype(BF)
        for h in range(2):
            mate_out[i, h] = value[:, columns[h]]
        mate_copies[i].append(send(mate_out.at[i, 0], mate_in.at[i, 0], mate))
    for i in range(2):
        mate_copies[i].append(send(mate_out.at[i, 1], mate_in.at[i, 1], mate))
    value = last_value(-3 + 6 * core).astype(BF)
    single_copies = []
    for h in range(2):
        comb_out[2, h] = value[:, columns[h]]
        single_copies.append(send(comb_out.at[2, h], comb_in.at[2, h], single))
    for offset in (-2, 2):
        sums[offset + 3] = last_value(offset)
    minus_copies, plus_copies = [], []
    for h in range(2):
        mate_copies[0][h].wait_recv()
        comb_out[0, h] = (sums[1, :, columns[h]] + mate_in[0, h].astype(F32)).astype(BF)
        minus_copies.append(send(comb_out.at[0, h], comb_in.at[0, h], k_minus))
        mate_copies[1][h].wait_recv()
        comb_out[1, h] = (sums[5, :, columns[h]] + mate_in[1, h].astype(F32)).astype(BF)
        plus_copies.append(send(comb_out.at[1, h], comb_in.at[1, h], k_plus))
        if h == 0:
            value = last_value(1 - 2 * core).astype(BF)
            for part in range(2):
                mate_out[2, part] = value[:, columns[part]]
                mate_copies[2].append(send(mate_out.at[2, part], mate_in.at[2, part], mate))
    sums[3] = last_value(0) + xblk[0].astype(F32)

    up_copy.wait()
    weight = weight_ref[...]
    g_plus, g_minus, g_mate, g_single = [], [], [], []
    kept = []
    for h in range(2):
        norm_h = norm[:, columns[h]]
        mate_copies[2][h].wait_recv()
        single_copies[h].wait_recv()
        total = sums[3, :, columns[h]] + mate_in[2, h].astype(F32) + comb_in[2, h].astype(F32)
        minus_copies[h].wait_recv()
        plus_copies[h].wait_recv()
        total = total + comb_in[0, h].astype(F32) + comb_in[1, h].astype(F32)
        aggregated = (norm_h * total).astype(BF)
        pre_act = (
            lax.dot_general(
                aggregated, weight, (((0,), (0,)), ((), ())), preferred_element_type=F32
            )
            + bias_ref[...]
        )
        gate = 1.0 / (1.0 + jnp.exp(-pre_act))
        rows = slice(h * HALF, (h + 1) * HALF)
        pre_grad = (
            up_v[rows, :].astype(F32) * (gate + pre_act * gate * (1.0 - gate))
        ).astype(BF)
        gblk[3, h] = (
            norm_h
            * lax.dot_general(
                weight, pre_grad, (((1,), (1,)), ((), ())), preferred_element_type=F32
            )
        ).astype(BF)
        g_plus.append(send(gblk.at[3, h], gblk.at[1, h], k_plus))
        g_minus.append(send(gblk.at[3, h], gblk.at[5, h], k_minus))
        g_mate.append(send(gblk.at[3, h], gblk.at[2 + 2 * core, h], mate))
        g_single.append(send(gblk.at[3, h], gblk.at[6 - 6 * core, h], single))
        hidden_ref[rows, :] = (pre_act * gate).astype(BF)
        kept.append((aggregated, pre_grad))

    local_weight = sum(jnp.dot(a, p, preferred_element_type=F32) for a, p in kept)
    local_bias = sum(jnp.sum(p.astype(F32), axis=0, keepdims=True) for _, p in kept)
    for i in range(4):
        for u in range(8):
            row = i * 32 + (u // 2) * 8
            lanes = slice((u % 2) * 128, (u % 2) * 128 + 128)
            w_send[i, u, 0:8] = local_weight[row : row + 8, lanes]
            w_send[i, u, 8:16] = jnp.broadcast_to(local_bias[:, lanes], (8, 128))
    w_y_copies = [
        send(w_send.at[lax.rem(y + j, 4)], w_y.at[y], y_peers[j - 1]) for j in range(1, 4)
    ]
    w_y[y] = w_send[y]

    def grad_product(source, groups):
        lhs = jnp.concatenate([gblk[g, h] for g in groups for h in range(2)], axis=1)
        rhs = jnp.concatenate(
            [
                jnp.concatenate(
                    [tile_v[table_s[g, a * 32 + source * 4 + b]] for b in range(4)], axis=1
                )
                for g in groups
                for a in range(4)
            ],
            axis=0,
        )
        return jnp.dot(lhs, rhs, preferred_element_type=F32)

    arrived(g_mate)
    for slot in range(8):
        sums[slot] = grad_product(source_block(slot), (3, 4 - 2 * core))
    passed = []
    for h in range(2):
        g_plus[h].wait_recv()
        passed.append(send(gblk.at[1, h], gblk.at[2 * core, h], mate))
        g_minus[h].wait_recv()
        passed.append(send(gblk.at[5, h], gblk.at[4 + 2 * core, h], mate))
    arrived(w_y_copies)
    w_z[...] = w_y[0] + w_y[1] + w_y[2] + w_y[3]
    w_z_copies = [
        send(w_z.at[lax.rem(z + j, 8)], w_zin.at[j - 1], z_peers[j - 1]) for j in range(1, 8)
    ]
    for slot in range(8):
        sums[slot] = sums[slot] + grad_product(source_block(slot), (1, 5))
    arrived(g_single + passed)

    def last_grad(slot):
        rest = (2 - 2 * core, 6 - 2 * core, 6 * core)
        return sums[slot] + grad_product(source_block(slot), rest)

    def first_hop(part):
        col_out[part, 2] = last_grad(part * 4 + 2).astype(BF)
        source = col_out.at[part, 2]
        to_plus = [send(source.at[low[i]], col_mid.at[part, 0, i], y_plus) for i in range(2)]
        to_minus = [send(source.at[high[i]], col_mid.at[part, 1, i], y_minus) for i in range(2)]
        return to_plus, to_minus

    def direct_hop(part):
        col_out[part, 1, FEAT // 2 :] = sums[part * 4 + 1, FEAT // 2 :].astype(BF)
        plus_b = send_parts(col_out.at[part, 1], col_in.at[part, 0], high, y_plus)
        col_out[part, 3, : FEAT // 2] = sums[part * 4 + 3, : FEAT // 2].astype(BF)
        minus_a = send_parts(col_out.at[part, 3], col_in.at[part, 1], low, y_minus)
        return plus_b, minus_a

    def relay_hop(part, to_plus, to_minus):
        plus_a, minus_b = [], []
        for i in range(2):
            to_plus[i].wait_recv()
            col_out[part, 1, low[i]] = (
                sums[part * 4 + 1, low[i]] + col_mid[part, 0, i].astype(F32)
            ).astype(BF)
            plus_a.append(
                send(col_out.at[part, 1, low[i]], col_in.at[part, 0, low[i]], y_plus)
            )
            to_minus[i].wait_recv()
            col_out[part, 3, high[i]] = (
                sums[part * 4 + 3, high[i]] + col_mid[part, 1, i].astype(F32)
            ).astype(BF)
            minus_b.append(
                send(col_out.at[part, 3, high[i]], col_in.at[part, 1, high[i]], y_minus)
            )
        return plus_a, minus_b

    far_first = first_hop(1)
    for slot in (5, 7):
        sums[slot] = last_grad(slot)
    far_plus_b, far_minus_a = direct_hop(1)
    for slot in (4, 1, 3):
        sums[slot] = last_grad(slot)
    arrived(w_z_copies)
    w_sum = w_z[z]
    for j in range(7):
        w_sum = w_sum + w_zin[j]
    w_x[...] = w_sum
    w_xall[x_place] = w_sum
    w_x_copies = [send(w_x, w_xall.at[x_place], x_peers[j - 1]) for j in range(1, 8)]
    far_plus_a, far_minus_b = relay_hop(1, *far_first)
    near_first = first_hop(0)
    near_plus_b, near_minus_a = direct_hop(0)
    own_grad = jnp.concatenate([gblk[3, 0], gblk[3, 1]], axis=1)
    sums[0] = last_grad(0) + own_grad.astype(F32)

    arrived(w_x_copies)
    w_sum = w_xall[0]
    for j in range(1, 8):
        w_sum = w_sum + w_xall[j]
    w_x_total[...] = w_sum
    w_zall[z] = w_sum
    w_g_copies = [send(w_x_total, w_zall.at[z], z_peers[j - 1]) for j in range(1, 8)]

    def partner_sum(part):
        xsum[part] = (
            sums[4, part] + col_in[1, 0, part].astype(F32) + col_in[1, 1, part].astype(F32)
        ).astype(BF)

    arrived(far_plus_b + far_minus_a)
    xs_a, xs_b = [], []
    for i in range(2):
        far_plus_a[i].wait_recv()
        partner_sum(low[i])
        xs_a.append(send(xsum.at[low[i]], xsum_transit.at[0, i], x_plus))
        far_minus_b[i].wait_recv()
        partner_sum(high[i])
        xs_b.append(send(xsum.at[high[i]], xsum_transit.at[1, i], x_minus))
    near_plus_a, near_minus_b = relay_hop(0, *near_first)
    xt_a, xt_b = [], []
    for i in range(2):
        xs_a[i].wait_recv()
        xt_a.append(send(xsum_transit.at[0, i], xsum_in.at[low[i]], x_plus))
        xs_b[i].wait_recv()
        xt_b.append(send(xsum_transit.at[1, i], xsum_in.at[high[i]], x_minus))
    arrived(w_g_copies)
    w_f_copies = [
        send(w_zall.at[:, pl.ds(0, 8)], w_all.at[y], y_peers[j - 1]) for j in range(1, 4)
    ]
    w_all[y] = w_zall[:, 0:8]
    scale = NODES ** (-0.5)
    bgrad_ref[:, 0:128] = w_zall[0, 8:9] * scale
    bgrad_ref[:, 128:256] = w_zall[1, 8:9] * scale
    arrived(near_plus_b + near_minus_a + near_plus_a + near_minus_b)
    column = sums[0] + col_in[0, 0].astype(F32) + col_in[0, 1].astype(F32)
    arrived(w_f_copies)
    for i in range(4):
        for u in range(8):
            row = i * 32 + (u // 2) * 8
            lane = (u % 2) * 128
            wgrad_ref[row : row + 8, lane : lane + 128] = w_all[i, u] * scale
    arrived(xt_a + xt_b)
    feature_grad = norm * (column + xsum_in[...].astype(F32))
    for i in range(4):
        fgrad_ref[i * TS : (i + 1) * TS, :] = feature_grad[:, i * TS : (i + 1) * TS].T.astype(BF)
    for copy in started:
        copy.wait_send()


def settle(*refs):
    for source, target in zip(refs[:4], refs[4:]):
        target[...] = source[...]


def on_device(
    features, degrees, tile_weights, tile_rows, tile_cols, tile_counts, weight, layer_bias, upstream
):
    vmem = pl.BlockSpec(memory_space=pltpu.VMEM)
    smem = pl.BlockSpec(memory_space=pltpu.SMEM)
    anywhere = pl.BlockSpec(memory_space=pl.ANY)
    blocks = lambda *lead: pltpu.VMEM((*lead, FEAT, ROWS), BF)
    parts = lambda *lead: pltpu.VMEM((*lead, 2, FEAT, HALF), BF)
    quarters = lambda *lead: pltpu.VMEM((*lead, QUARTER, ROWS), BF)
    units = lambda *lead: pltpu.VMEM((*lead, 16, 128), F32)
    shapes = [
        jax.ShapeDtypeStruct((ROWS, HID), BF),
        jax.ShapeDtypeStruct((ROWS, FEAT), BF),
        jax.ShapeDtypeStruct((FEAT, HID), F32),
        jax.ShapeDtypeStruct((1, HID), F32),
    ]
    results = pl.pallas_call(
        kernel,
        in_specs=[smem, smem, anywhere, anywhere, vmem, anywhere, vmem, vmem, anywhere],
        out_specs=[vmem, vmem, vmem, vmem],
        out_shape=shapes,
        scratch_shapes=[
            pltpu.VMEM((ROWS, FEAT), BF),
            pltpu.VMEM((ROWS, HID), BF),
            pltpu.VMEM((SLOTS + 1, TS, TS), BF),
            pltpu.VMEM((SLOTS + 1, TS, TS), BF),
            pltpu.VMEM((8, FEAT, ROWS), F32),
            blocks(8),
            quarters(2, 2),
            parts(3),
            parts(3),
            parts(3),
            parts(3),
            parts(7),
            blocks(2, 4),
            quarters(2, 2, 2),
            blocks(2, 2),
            blocks(),
            quarters(2, 2),
            blocks(),
            units(4, 8),
            units(4, 8),
            units(8),
            units(7),
            units(),
            units(8),
            units(),
            units(8),
            pltpu.VMEM((4, 8, 8, 128), F32),
            pltpu.VMEM((8, 128), jnp.int32),
            pltpu.SMEM((8, 128), jnp.int32),
            pltpu.SMEM((1, 1), jnp.int32),
            pltpu.SemaphoreType.DMA((4,)),
            pltpu.SemaphoreType.DMA((CHUNKS,)),
            pltpu.SemaphoreType.DMA((N_COPIES,)),
            pltpu.SemaphoreType.DMA((N_COPIES,)),
        ],
        compiler_params=pltpu.CompilerParams(
            collective_id=0, has_side_effects=True, vmem_limit_bytes=56 << 20
        ),
        name="layer",
    )(
        tile_rows,
        tile_cols,
        tile_counts,
        features,
        degrees.reshape(1, ROWS),
        tile_weights.reshape(SLOTS, TS, TS),
        weight,
        layer_bias.reshape(1, HID),
        upstream,
    )
    hidden, feature_grad, weight_grad, bias_grad = pl.pallas_call(
        settle, in_specs=[vmem] * 4, out_specs=[vmem] * 4, out_shape=shapes, name="settle"
    )(*results)
    return hidden, feature_grad, weight_grad, bias_grad.reshape(HID)


def solution(mesh):
    placed = (
        P(("rep", "blk"), None),
        P(("rep", "blk")),
        P("rep", "blk", None, None, None),
        P("rep", "blk", None),
        P("rep", "blk", None),
        P("rep", "blk"),
        P(),
        P(),
        P(("rep", "blk"), None),
    )
    return jax.shard_map(
        on_device,
        mesh=mesh,
        in_specs=placed,
        out_specs=(P(("rep", "blk"), None), P(("rep", "blk"), None), P(), P()),
        check_vma=False,
    )
```

```python
import itertools

import jax
import jax.numpy as jnp
from jax import lax
from jax.experimental import pallas as pl
from jax.experimental.pallas import tpu as pltpu
from jax.sharding import PartitionSpec as P

BF = jnp.bfloat16
F32 = jnp.float32
MESH = pl.DeviceIdType.MESH
SLOTS = 320
TS = 128
ROWS = 512
HALF = 256
FEAT = 128
HID = 256
QUARTER = 32
N_COPIES = 128
CHUNKS = 10
NODES = 131072


def kernel(
    rows_s,
    cols_s,
    count_hbm,
    feat_hbm,
    deg_ref,
    tiles_hbm,
    weight_ref,
    bias_ref,
    up_hbm,
    hidden_ref,
    fgrad_ref,
    wgrad_ref,
    bgrad_ref,
    feat_v,
    up_v,
    tile_v,
    tile_t,
    sums,
    xblk,
    mate_out,
    mate_in,
    comb_out,
    comb_in,
    gblk,
    col_out,
    col_mid,
    col_in,
    xsum,
    xsum_in,
    w_send,
    w_y,
    w_z,
    w_zin,
    w_x,
    w_xall,
    w_x_total,
    w_zall,
    w_all,
    table_v,
    table_s,
    count_s,
    local_sem,
    tile_sem,
    send_sem,
    recv_sem,
):
    rep = lax.axis_index("rep")
    blk = lax.axis_index("blk")
    y = lax.div(rep, 2)
    xh = lax.rem(rep, 2)
    z = lax.div(blk, 4)
    xl = lax.rem(lax.div(blk, 2), 2)
    core = lax.rem(blk, 2)
    y_plus = (lax.rem(rep + 2, 8), blk)
    y_minus = (lax.rem(rep + 6, 8), blk)
    partner = (2 * y + 1 - xh, blk)
    mate = (rep, blk + 1 - 2 * core)
    k_plus = (rep, lax.rem(blk + 2, 32))
    k_minus = (rep, lax.rem(blk + 30, 32))
    single = (rep, lax.rem(blk + 29 + 6 * core, 32))
    y_peers = [(lax.rem(rep + 2 * j, 8), blk) for j in range(1, 4)]
    z_peers = [(rep, lax.rem(blk + 4 * j, 32)) for j in range(1, 8)]
    x_peers = [
        (
            2 * y + lax.rem(xh + j // 4, 2),
            4 * z + 2 * lax.rem(xl + (j // 2) % 2, 2) + lax.rem(core + j % 2, 2),
        )
        for j in range(1, 8)
    ]
    x_place = xh * 4 + xl * 2 + core

    ids = itertools.count()
    started = []

    def send(src, dst, device):
        at = next(ids)
        copy = pltpu.make_async_remote_copy(
            src_ref=src,
            dst_ref=dst,
            send_sem=send_sem.at[at],
            recv_sem=recv_sem.at[at],
            device_id=device,
            device_id_type=MESH,
        )
        copy.start()
        started.append(copy)
        return copy

    low = [pl.ds(i * QUARTER, QUARTER) for i in range(2)]
    high = [pl.ds(FEAT // 2 + i * QUARTER, QUARTER) for i in range(2)]

    def send_parts(src, dst, parts, device):
        return [send(src.at[part], dst.at[part], device) for part in parts]

    def arrived(copies):
        for copy in copies:
            copy.wait_recv()

    feat_copy = pltpu.make_async_copy(feat_hbm, feat_v, local_sem.at[0])
    feat_copy.start()
    count_copy = pltpu.make_async_copy(count_hbm, count_s, local_sem.at[3])
    count_copy.start()
    per_chunk = SLOTS // CHUNKS
    tile_copies = [
        pltpu.make_async_copy(
            tiles_hbm.at[pl.ds(i * per_chunk, per_chunk)],
            tile_v.at[pl.ds(i * per_chunk, per_chunk)],
            tile_sem.at[i],
        )
        for i in range(CHUNKS)
    ]
    for copy in tile_copies:
        copy.start()
    up_copy = pltpu.make_async_copy(up_hbm, up_v, local_sem.at[1])
    up_copy.start()

    barrier = pltpu.get_barrier_semaphore()
    peers = y_peers + z_peers + x_peers + [k_plus, k_minus, single]
    for peer in peers:
        pl.semaphore_signal(barrier, inc=1, device_id=peer, device_id_type=MESH)

    norm = 1.0 / jnp.sqrt(deg_ref[...].astype(F32) + 1.0)
    feat_copy.wait()
    features = feat_v[...].astype(F32)
    own_x = (norm * jnp.concatenate([features[i * TS : (i + 1) * TS].T for i in range(4)], axis=1)).astype(BF)
    xblk[0] = own_x
    pl.semaphore_wait(barrier, len(peers))

    own = xblk.at[0]
    far_a, far_b = [], []
    for i in range(2):
        far_a.append(send(own.at[low[i]], xblk.at[4, low[i]], partner))
        far_b.append(send(own.at[high[i]], xblk.at[4, high[i]], partner))
    own_pa, own_mb, own_pb, own_ma = [], [], [], []
    for i in range(2):
        own_pa.append(send(own.at[low[i]], xblk.at[3, low[i]], y_plus))
        own_mb.append(send(own.at[high[i]], xblk.at[1, high[i]], y_minus))
    for i in range(2):
        own_pb.append(send(own.at[high[i]], xblk.at[3, high[i]], y_plus))
        own_ma.append(send(own.at[low[i]], xblk.at[1, low[i]], y_minus))

    count_copy.wait()
    count = count_s[0, 0]
    places = (
        lax.broadcasted_iota(jnp.int32, (8, 128), 0) * 128
        + lax.broadcasted_iota(jnp.int32, (8, 128), 1)
    )

    def add_slots(i, table):
        for u in range(8):
            t = i * 8 + u
            h = rows_s[0, 0, t]
            gap = (lax.shift_right_logical(h, 2) - blk + 35) & 31
            key = (gap << 7) + ((h & 3) << 5) + cols_s[0, 0, t]
            key = jnp.where(t < count, key, 4096)
            table = jnp.where(places == key, t, table)
        return table

    table_v[...] = lax.fori_loop(0, SLOTS // 8, add_slots, jnp.full((8, 128), SLOTS, jnp.int32))
    table_copy = pltpu.make_async_copy(table_v, table_s, local_sem.at[2])
    table_copy.start()
    tile_v[SLOTS] = jnp.zeros((TS, TS), BF)
    tile_t[SLOTS] = jnp.zeros((TS, TS), BF)

    def transpose_chunk(chunk):
        tile_copies[chunk].wait()

        def some(i, carry):
            for u in range(16):
                t = chunk * per_chunk + i * 16 + u
                tile_t[t] = tile_v[t].T
            return carry

        lax.fori_loop(0, per_chunk // 16, some, 0)

    for chunk in range(2):
        transpose_chunk(chunk)
    two_a, two_b = [], []
    for i in range(2):
        own_pa[i].wait_recv()
        two_a.append(send(xblk.at[3, low[i]], xblk.at[2, low[i]], y_plus))
        own_mb[i].wait_recv()
        two_b.append(send(xblk.at[1, high[i]], xblk.at[2, high[i]], y_minus))
    for chunk in range(2, 4):
        transpose_chunk(chunk)
    far_pa, far_ma, far_pb, far_mb = [], [], [], []
    for i in range(2):
        far_a[i].wait_recv()
        far_pa.append(send(xblk.at[4, low[i]], xblk.at[7, low[i]], y_plus))
        far_b[i].wait_recv()
        far_mb.append(send(xblk.at[4, high[i]], xblk.at[5, high[i]], y_minus))
        far_ma.append(send(xblk.at[4, low[i]], xblk.at[5, low[i]], y_minus))
        far_pb.append(send(xblk.at[4, high[i]], xblk.at[7, high[i]], y_plus))
        if i == 0:
            for chunk in range(4, 6):
                transpose_chunk(chunk)
    for chunk in range(6, CHUNKS):
        transpose_chunk(chunk)
    far2_a, far2_b = [], []
    for i in range(2):
        far_pa[i].wait_recv()
        far2_a.append(send(xblk.at[7, low[i]], xblk.at[6, low[i]], y_plus))
        far_mb[i].wait_recv()
        far2_b.append(send(xblk.at[5, high[i]], xblk.at[6, high[i]], y_minus))
    table_copy.wait()

    def source_block(slot):
        return lax.rem(y + slot % 4, 4) * 2 + lax.rem(xh + slot // 4, 2)

    def value_product(group, slots):
        lhs = jnp.concatenate([xblk[s] for s in slots], axis=1)
        rhs = jnp.concatenate(
            [
                jnp.concatenate(
                    [tile_t[table_s[group, a * 32 + source_block(s) * 4 + b]] for a in range(4)],
                    axis=1,
                )
                for s in slots
                for b in range(4)
            ],
            axis=0,
        )
        return jnp.dot(lhs, rhs, preferred_element_type=F32)

    arrived(own_pb + own_ma)
    for group in range(7):
        sums[group] = value_product(group, (0, 1, 3))
    arrived(two_a + two_b)
    for group in range(7):
        sums[group] = sums[group] + value_product(group, (2, 4))
    arrived(far_pb + far_ma)
    for group in range(7):
        sums[group] = sums[group] + value_product(group, (5, 7))
    arrived(far2_a + far2_b)

    def last_value(offset):
        group = offset + 3
        return sums[group] + value_product(group, (6,))

    columns = [slice(h * HALF, (h + 1) * HALF) for h in range(2)]
    mate_copies = [[], [], []]
    for i, offset in enumerate((-1 - 2 * core, 3 - 2 * core)):
        value = last_value(offset).astype(BF)
        for h in range(2):
            mate_out[i, h] = value[:, columns[h]]
        mate_copies[i].append(send(mate_out.at[i, 0], mate_in.at[i, 0], mate))
    for i in range(2):
        mate_copies[i].append(send(mate_out.at[i, 1], mate_in.at[i, 1], mate))
    value = last_value(-3 + 6 * core).astype(BF)
    single_copies = []
    for h in range(2):
        comb_out[2, h] = value[:, columns[h]]
        single_copies.append(send(comb_out.at[2, h], comb_in.at[2, h], single))
    for offset in (-2, 2):
        sums[offset + 3] = last_value(offset)
    minus_copies, plus_copies = [], []
    for h in range(2):
        mate_copies[0][h].wait_recv()
        comb_out[0, h] = (sums[1, :, columns[h]] + mate_in[0, h].astype(F32)).astype(BF)
        minus_copies.append(send(comb_out.at[0, h], comb_in.at[0, h], k_minus))
        mate_copies[1][h].wait_recv()
        comb_out[1, h] = (sums[5, :, columns[h]] + mate_in[1, h].astype(F32)).astype(BF)
        plus_copies.append(send(comb_out.at[1, h], comb_in.at[1, h], k_plus))
        if h == 0:
            value = last_value(1 - 2 * core).astype(BF)
            for part in range(2):
                mate_out[2, part] = value[:, columns[part]]
                mate_copies[2].append(send(mate_out.at[2, part], mate_in.at[2, part], mate))
    sums[3] = last_value(0) + xblk[0].astype(F32)

    up_copy.wait()
    weight = weight_ref[...]
    g_plus, g_minus, g_mate, g_single = [], [], [], []
    kept = []
    for h in range(2):
        norm_h = norm[:, columns[h]]
        mate_copies[2][h].wait_recv()
        single_copies[h].wait_recv()
        total = sums[3, :, columns[h]] + mate_in[2, h].astype(F32) + comb_in[2, h].astype(F32)
        minus_copies[h].wait_recv()
        plus_copies[h].wait_recv()
        total = total + comb_in[0, h].astype(F32) + comb_in[1, h].astype(F32)
        aggregated = (norm_h * total).astype(BF)
        pre_act = (
            lax.dot_general(
                aggregated, weight, (((0,), (0,)), ((), ())), preferred_element_type=F32
            )
            + bias_ref[...]
        )
        gate = 1.0 / (1.0 + jnp.exp(-pre_act))
        rows = slice(h * HALF, (h + 1) * HALF)
        pre_grad = (
            up_v[rows, :].astype(F32) * (gate + pre_act * gate * (1.0 - gate))
        ).astype(BF)
        gblk[3, h] = (
            norm_h
            * lax.dot_general(
                weight, pre_grad, (((1,), (1,)), ((), ())), preferred_element_type=F32
            )
        ).astype(BF)
        g_plus.append(send(gblk.at[3, h], gblk.at[1, h], k_plus))
        g_minus.append(send(gblk.at[3, h], gblk.at[5, h], k_minus))
        g_mate.append(send(gblk.at[3, h], gblk.at[2 + 2 * core, h], mate))
        g_single.append(send(gblk.at[3, h], gblk.at[6 - 6 * core, h], single))
        hidden_ref[rows, :] = (pre_act * gate).astype(BF)
        kept.append((aggregated, pre_grad))

    local_weight = sum(jnp.dot(a, p, preferred_element_type=F32) for a, p in kept)
    local_bias = sum(jnp.sum(p.astype(F32), axis=0, keepdims=True) for _, p in kept)
    for i in range(4):
        for u in range(8):
            row = i * 32 + (u // 2) * 8
            lanes = slice((u % 2) * 128, (u % 2) * 128 + 128)
            w_send[i, u, 0:8] = local_weight[row : row + 8, lanes]
            w_send[i, u, 8:16] = jnp.broadcast_to(local_bias[:, lanes], (8, 128))
    w_y_copies = [
        send(w_send.at[lax.rem(y + j, 4)], w_y.at[y], y_peers[j - 1]) for j in range(1, 4)
    ]
    w_y[y] = w_send[y]

    def grad_product(source, groups):
        lhs = jnp.concatenate([gblk[g, h] for g in groups for h in range(2)], axis=1)
        rhs = jnp.concatenate(
            [
                jnp.concatenate(
                    [tile_v[table_s[g, a * 32 + source * 4 + b]] for b in range(4)], axis=1
                )
                for g in groups
                for a in range(4)
            ],
            axis=0,
        )
        return jnp.dot(lhs, rhs, preferred_element_type=F32)

    arrived(g_mate)
    for slot in range(8):
        sums[slot] = grad_product(source_block(slot), (3, 4 - 2 * core))
    passed = []
    for h in range(2):
        g_plus[h].wait_recv()
        passed.append(send(gblk.at[1, h], gblk.at[2 * core, h], mate))
        g_minus[h].wait_recv()
        passed.append(send(gblk.at[5, h], gblk.at[4 + 2 * core, h], mate))
    arrived(w_y_copies)
    w_z[...] = w_y[0] + w_y[1] + w_y[2] + w_y[3]
    w_z_copies = [
        send(w_z.at[lax.rem(z + j, 8)], w_zin.at[j - 1], z_peers[j - 1]) for j in range(1, 8)
    ]
    for slot in range(8):
        sums[slot] = sums[slot] + grad_product(source_block(slot), (1, 5))
    arrived(g_single + passed)

    def last_grad(slot):
        rest = (2 - 2 * core, 6 - 2 * core, 6 * core)
        return sums[slot] + grad_product(source_block(slot), rest)

    def first_hop(part):
        col_out[part, 2] = last_grad(part * 4 + 2).astype(BF)
        source = col_out.at[part, 2]
        to_plus = [send(source.at[low[i]], col_mid.at[part, 0, i], y_plus) for i in range(2)]
        to_minus = [send(source.at[high[i]], col_mid.at[part, 1, i], y_minus) for i in range(2)]
        return to_plus, to_minus

    def direct_hop(part):
        col_out[part, 1, FEAT // 2 :] = sums[part * 4 + 1, FEAT // 2 :].astype(BF)
        plus_b = send_parts(col_out.at[part, 1], col_in.at[part, 0], high, y_plus)
        col_out[part, 3, : FEAT // 2] = sums[part * 4 + 3, : FEAT // 2].astype(BF)
        minus_a = send_parts(col_out.at[part, 3], col_in.at[part, 1], low, y_minus)
        return plus_b, minus_a

    def relay_hop(part, to_plus, to_minus):
        plus_a, minus_b = [], []
        for i in range(2):
            to_plus[i].wait_recv()
            col_out[part, 1, low[i]] = (
                sums[part * 4 + 1, low[i]] + col_mid[part, 0, i].astype(F32)
            ).astype(BF)
            plus_a.append(
                send(col_out.at[part, 1, low[i]], col_in.at[part, 0, low[i]], y_plus)
            )
            to_minus[i].wait_recv()
            col_out[part, 3, high[i]] = (
                sums[part * 4 + 3, high[i]] + col_mid[part, 1, i].astype(F32)
            ).astype(BF)
            minus_b.append(
                send(col_out.at[part, 3, high[i]], col_in.at[part, 1, high[i]], y_minus)
            )
        return plus_a, minus_b

    far_first = first_hop(1)
    for slot in (5, 7):
        sums[slot] = last_grad(slot)
    far_plus_b, far_minus_a = direct_hop(1)
    for slot in (4, 1, 3):
        sums[slot] = last_grad(slot)
    arrived(w_z_copies)
    w_sum = w_z[z]
    for j in range(7):
        w_sum = w_sum + w_zin[j]
    w_x[...] = w_sum
    w_xall[x_place] = w_sum
    w_x_copies = [send(w_x, w_xall.at[x_place], x_peers[j - 1]) for j in range(1, 8)]
    far_plus_a, far_minus_b = relay_hop(1, *far_first)
    near_first = first_hop(0)
    near_plus_b, near_minus_a = direct_hop(0)
    own_grad = jnp.concatenate([gblk[3, 0], gblk[3, 1]], axis=1)
    sums[0] = last_grad(0) + own_grad.astype(F32)

    arrived(w_x_copies)
    w_sum = w_xall[0]
    for j in range(1, 8):
        w_sum = w_sum + w_xall[j]
    w_x_total[...] = w_sum
    w_zall[z] = w_sum
    w_g_copies = [send(w_x_total, w_zall.at[z], z_peers[j - 1]) for j in range(1, 8)]

    def partner_sum(part):
        xsum[part] = (
            sums[4, part] + col_in[1, 0, part].astype(F32) + col_in[1, 1, part].astype(F32)
        ).astype(BF)

    arrived(far_plus_b + far_minus_a)
    xs_a, xs_b = [], []
    for i in range(2):
        far_plus_a[i].wait_recv()
        partner_sum(low[i])
        xs_a.append(send(xsum.at[low[i]], xsum_in.at[low[i]], partner))
        far_minus_b[i].wait_recv()
        partner_sum(high[i])
        xs_b.append(send(xsum.at[high[i]], xsum_in.at[high[i]], partner))
    near_plus_a, near_minus_b = relay_hop(0, *near_first)
    arrived(w_g_copies)
    w_f_copies = [
        send(w_zall.at[:, pl.ds(0, 8)], w_all.at[y], y_peers[j - 1]) for j in range(1, 4)
    ]
    w_all[y] = w_zall[:, 0:8]
    scale = NODES ** (-0.5)
    bgrad_ref[:, 0:128] = w_zall[0, 8:9] * scale
    bgrad_ref[:, 128:256] = w_zall[1, 8:9] * scale
    arrived(near_plus_b + near_minus_a + near_plus_a + near_minus_b)
    column = sums[0] + col_in[0, 0].astype(F32) + col_in[0, 1].astype(F32)
    arrived(w_f_copies)
    for i in range(4):
        for u in range(8):
            row = i * 32 + (u // 2) * 8
            lane = (u % 2) * 128
            wgrad_ref[row : row + 8, lane : lane + 128] = w_all[i, u] * scale
    arrived(xs_a + xs_b)
    feature_grad = norm * (column + xsum_in[...].astype(F32))
    for i in range(4):
        fgrad_ref[i * TS : (i + 1) * TS, :] = feature_grad[:, i * TS : (i + 1) * TS].T.astype(BF)
    for copy in started:
        copy.wait_send()


def settle(*refs):
    for source, target in zip(refs[:4], refs[4:]):
        target[...] = source[...]


def on_device(
    features, degrees, tile_weights, tile_rows, tile_cols, tile_counts, weight, layer_bias, upstream
):
    vmem = pl.BlockSpec(memory_space=pltpu.VMEM)
    smem = pl.BlockSpec(memory_space=pltpu.SMEM)
    anywhere = pl.BlockSpec(memory_space=pl.ANY)
    blocks = lambda *lead: pltpu.VMEM((*lead, FEAT, ROWS), BF)
    parts = lambda *lead: pltpu.VMEM((*lead, 2, FEAT, HALF), BF)
    quarters = lambda *lead: pltpu.VMEM((*lead, QUARTER, ROWS), BF)
    units = lambda *lead: pltpu.VMEM((*lead, 16, 128), F32)
    shapes = [
        jax.ShapeDtypeStruct((ROWS, HID), BF),
        jax.ShapeDtypeStruct((ROWS, FEAT), BF),
        jax.ShapeDtypeStruct((FEAT, HID), F32),
        jax.ShapeDtypeStruct((1, HID), F32),
    ]
    results = pl.pallas_call(
        kernel,
        in_specs=[smem, smem, anywhere, anywhere, vmem, anywhere, vmem, vmem, anywhere],
        out_specs=[vmem, vmem, vmem, vmem],
        out_shape=shapes,
        scratch_shapes=[
            pltpu.VMEM((ROWS, FEAT), BF),
            pltpu.VMEM((ROWS, HID), BF),
            pltpu.VMEM((SLOTS + 1, TS, TS), BF),
            pltpu.VMEM((SLOTS + 1, TS, TS), BF),
            pltpu.VMEM((8, FEAT, ROWS), F32),
            blocks(8),
            parts(3),
            parts(3),
            parts(3),
            parts(3),
            parts(7),
            blocks(2, 4),
            quarters(2, 2, 2),
            blocks(2, 2),
            blocks(),
            blocks(),
            units(4, 8),
            units(4, 8),
            units(8),
            units(7),
            units(),
            units(8),
            units(),
            units(8),
            pltpu.VMEM((4, 8, 8, 128), F32),
            pltpu.VMEM((8, 128), jnp.int32),
            pltpu.SMEM((8, 128), jnp.int32),
            pltpu.SMEM((1, 1), jnp.int32),
            pltpu.SemaphoreType.DMA((4,)),
            pltpu.SemaphoreType.DMA((CHUNKS,)),
            pltpu.SemaphoreType.DMA((N_COPIES,)),
            pltpu.SemaphoreType.DMA((N_COPIES,)),
        ],
        compiler_params=pltpu.CompilerParams(
            collective_id=0, has_side_effects=True, vmem_limit_bytes=56 << 20
        ),
        name="layer",
    )(
        tile_rows,
        tile_cols,
        tile_counts,
        features,
        degrees.reshape(1, ROWS),
        tile_weights.reshape(SLOTS, TS, TS),
        weight,
        layer_bias.reshape(1, HID),
        upstream,
    )
    hidden, feature_grad, weight_grad, bias_grad = pl.pallas_call(
        settle, in_specs=[vmem] * 4, out_specs=[vmem] * 4, out_shape=shapes, name="settle"
    )(*results)
    return hidden, feature_grad, weight_grad, bias_grad.reshape(HID)


def solution(mesh):
    placed = (
        P(("rep", "blk"), None),
        P(("rep", "blk")),
        P("rep", "blk", None, None, None),
        P("rep", "blk", None),
        P("rep", "blk", None),
        P("rep", "blk"),
        P(),
        P(),
        P(("rep", "blk"), None),
    )
    return jax.shard_map(
        on_device,
        mesh=mesh,
        in_specs=placed,
        out_specs=(P(("rep", "blk"), None), P(("rep", "blk"), None), P(), P()),
        check_vma=False,
    )
```

```python
import itertools

import jax
import jax.numpy as jnp
from jax import lax
from jax.experimental import pallas as pl
from jax.experimental.pallas import tpu as pltpu
from jax.sharding import PartitionSpec as P

BF = jnp.bfloat16
F32 = jnp.float32
MESH = pl.DeviceIdType.MESH
SLOTS = 320
TS = 128
ROWS = 512
HALF = 256
FEAT = 128
HID = 256
QUARTER = 32
N_COPIES = 128
CHUNKS = 10
NODES = 131072


def kernel(
    rows_s,
    cols_s,
    count_hbm,
    feat_hbm,
    deg_ref,
    tiles_hbm,
    weight_ref,
    bias_ref,
    up_hbm,
    hidden_hbm,
    fgrad_ref,
    wgrad_ref,
    bgrad_ref,
    hidden_v,
    feat_v,
    up_v,
    tile_v,
    tile_t,
    sums,
    xblk,
    mate_out,
    mate_in,
    comb_out,
    comb_in,
    gblk,
    col_out,
    col_mid,
    col_in,
    xsum,
    xsum_in,
    w_send,
    w_y,
    w_z,
    w_zin,
    w_x,
    w_xall,
    w_x_total,
    w_zall,
    w_all,
    table_v,
    table_s,
    count_s,
    local_sem,
    tile_sem,
    send_sem,
    recv_sem,
):
    rep = lax.axis_index("rep")
    blk = lax.axis_index("blk")
    y = lax.div(rep, 2)
    xh = lax.rem(rep, 2)
    z = lax.div(blk, 4)
    xl = lax.rem(lax.div(blk, 2), 2)
    core = lax.rem(blk, 2)
    y_plus = (lax.rem(rep + 2, 8), blk)
    y_minus = (lax.rem(rep + 6, 8), blk)
    partner = (2 * y + 1 - xh, blk)
    mate = (rep, blk + 1 - 2 * core)
    k_plus = (rep, lax.rem(blk + 2, 32))
    k_minus = (rep, lax.rem(blk + 30, 32))
    single = (rep, lax.rem(blk + 29 + 6 * core, 32))
    y_peers = [(lax.rem(rep + 2 * j, 8), blk) for j in range(1, 4)]
    z_peers = [(rep, lax.rem(blk + 4 * j, 32)) for j in range(1, 8)]
    x_peers = [
        (
            2 * y + lax.rem(xh + j // 4, 2),
            4 * z + 2 * lax.rem(xl + (j // 2) % 2, 2) + lax.rem(core + j % 2, 2),
        )
        for j in range(1, 8)
    ]
    x_place = xh * 4 + xl * 2 + core

    ids = itertools.count()
    started = []

    def send(src, dst, device):
        at = next(ids)
        copy = pltpu.make_async_remote_copy(
            src_ref=src,
            dst_ref=dst,
            send_sem=send_sem.at[at],
            recv_sem=recv_sem.at[at],
            device_id=device,
            device_id_type=MESH,
        )
        copy.start()
        started.append(copy)
        return copy

    low = [pl.ds(i * QUARTER, QUARTER) for i in range(2)]
    high = [pl.ds(FEAT // 2 + i * QUARTER, QUARTER) for i in range(2)]

    def send_parts(src, dst, parts, device):
        return [send(src.at[part], dst.at[part], device) for part in parts]

    def arrived(copies):
        for copy in copies:
            copy.wait_recv()

    barrier = pltpu.get_barrier_semaphore()
    peers = z_peers + y_peers + x_peers + [k_plus, k_minus, single]
    for peer in peers:
        pl.semaphore_signal(barrier, inc=1, device_id=peer, device_id_type=MESH)

    feat_copy = pltpu.make_async_copy(feat_hbm, feat_v, local_sem.at[0])
    feat_copy.start()
    count_copy = pltpu.make_async_copy(count_hbm, count_s, local_sem.at[3])
    count_copy.start()
    per_chunk = SLOTS // CHUNKS
    tile_copies = [
        pltpu.make_async_copy(
            tiles_hbm.at[pl.ds(i * per_chunk, per_chunk)],
            tile_v.at[pl.ds(i * per_chunk, per_chunk)],
            tile_sem.at[i],
        )
        for i in range(CHUNKS)
    ]
    for copy in tile_copies:
        copy.start()
    up_copy = pltpu.make_async_copy(up_hbm, up_v, local_sem.at[1])
    up_copy.start()

    norm = 1.0 / jnp.sqrt(deg_ref[...].astype(F32) + 1.0)
    feat_copy.wait()
    features = feat_v[...].astype(F32)
    own_x = (norm * jnp.concatenate([features[i * TS : (i + 1) * TS].T for i in range(4)], axis=1)).astype(BF)
    xblk[0] = own_x
    pl.semaphore_wait(barrier, len(peers))

    own = xblk.at[0]
    far_a, far_b = [], []
    for i in range(2):
        far_a.append(send(own.at[low[i]], xblk.at[4, low[i]], partner))
        far_b.append(send(own.at[high[i]], xblk.at[4, high[i]], partner))
    own_pa, own_mb, own_pb, own_ma = [], [], [], []
    for i in range(2):
        own_pa.append(send(own.at[low[i]], xblk.at[3, low[i]], y_plus))
        own_mb.append(send(own.at[high[i]], xblk.at[1, high[i]], y_minus))
    for i in range(2):
        own_pb.append(send(own.at[high[i]], xblk.at[3, high[i]], y_plus))
        own_ma.append(send(own.at[low[i]], xblk.at[1, low[i]], y_minus))

    count_copy.wait()
    count = count_s[0, 0]
    places = (
        lax.broadcasted_iota(jnp.int32, (8, 128), 0) * 128
        + lax.broadcasted_iota(jnp.int32, (8, 128), 1)
    )

    def add_slots(i, table):
        for u in range(8):
            t = i * 8 + u
            h = rows_s[0, 0, t]
            gap = (lax.shift_right_logical(h, 2) - blk + 35) & 31
            key = (gap << 7) + ((h & 3) << 5) + cols_s[0, 0, t]
            key = jnp.where(t < count, key, 4096)
            table = jnp.where(places == key, t, table)
        return table

    table_v[...] = lax.fori_loop(0, SLOTS // 8, add_slots, jnp.full((8, 128), SLOTS, jnp.int32))
    table_copy = pltpu.make_async_copy(table_v, table_s, local_sem.at[2])
    table_copy.start()
    tile_v[SLOTS] = jnp.zeros((TS, TS), BF)
    tile_t[SLOTS] = jnp.zeros((TS, TS), BF)

    def transpose_chunk(chunk):
        tile_copies[chunk].wait()

        def some(i, carry):
            for u in range(16):
                t = chunk * per_chunk + i * 16 + u
                tile_t[t] = tile_v[t].T
            return carry

        lax.fori_loop(0, per_chunk // 16, some, 0)

    for chunk in range(2):
        transpose_chunk(chunk)
    two_a, two_b = [], []
    for i in range(2):
        own_pa[i].wait_recv()
        two_a.append(send(xblk.at[3, low[i]], xblk.at[2, low[i]], y_plus))
        own_mb[i].wait_recv()
        two_b.append(send(xblk.at[1, high[i]], xblk.at[2, high[i]], y_minus))
    for chunk in range(2, 4):
        transpose_chunk(chunk)
    far_pa, far_ma, far_pb, far_mb = [], [], [], []
    for i in range(2):
        far_a[i].wait_recv()
        far_pa.append(send(xblk.at[4, low[i]], xblk.at[7, low[i]], y_plus))
        far_b[i].wait_recv()
        far_mb.append(send(xblk.at[4, high[i]], xblk.at[5, high[i]], y_minus))
        far_ma.append(send(xblk.at[4, low[i]], xblk.at[5, low[i]], y_minus))
        far_pb.append(send(xblk.at[4, high[i]], xblk.at[7, high[i]], y_plus))
        if i == 0:
            for chunk in range(4, 6):
                transpose_chunk(chunk)
    for chunk in range(6, CHUNKS):
        transpose_chunk(chunk)
    far2_a, far2_b = [], []
    for i in range(2):
        far_pa[i].wait_recv()
        far2_a.append(send(xblk.at[7, low[i]], xblk.at[6, low[i]], y_plus))
        far_mb[i].wait_recv()
        far2_b.append(send(xblk.at[5, high[i]], xblk.at[6, high[i]], y_minus))
    table_copy.wait()

    def source_block(slot):
        return lax.rem(y + slot % 4, 4) * 2 + lax.rem(xh + slot // 4, 2)

    def value_product(group, slots):
        lhs = jnp.concatenate([xblk[s] for s in slots], axis=1)
        rhs = jnp.concatenate(
            [
                jnp.concatenate(
                    [tile_t[table_s[group, a * 32 + source_block(s) * 4 + b]] for a in range(4)],
                    axis=1,
                )
                for s in slots
                for b in range(4)
            ],
            axis=0,
        )
        return jnp.dot(lhs, rhs, preferred_element_type=F32)

    arrived(own_pb + own_ma)
    for group in range(7):
        sums[group] = value_product(group, (0, 1, 3))
    arrived(two_a + two_b)
    for group in range(7):
        sums[group] = sums[group] + value_product(group, (2, 4))
    arrived(far_pb + far_ma)
    for group in range(7):
        sums[group] = sums[group] + value_product(group, (5, 7))
    arrived(far2_a + far2_b)

    def last_value(offset):
        group = offset + 3
        return sums[group] + value_product(group, (6,))

    columns = [slice(h * HALF, (h + 1) * HALF) for h in range(2)]
    mate_copies = [[], [], []]
    for i, offset in enumerate((-1 - 2 * core, 3 - 2 * core)):
        value = last_value(offset).astype(BF)
        for h in range(2):
            mate_out[i, h] = value[:, columns[h]]
        mate_copies[i].append(send(mate_out.at[i, 0], mate_in.at[i, 0], mate))
    for i in range(2):
        mate_copies[i].append(send(mate_out.at[i, 1], mate_in.at[i, 1], mate))
    value = last_value(-3 + 6 * core).astype(BF)
    single_copies = []
    for h in range(2):
        comb_out[2, h] = value[:, columns[h]]
        single_copies.append(send(comb_out.at[2, h], comb_in.at[2, h], single))
    for offset in (-2, 2):
        sums[offset + 3] = last_value(offset)
    minus_copies, plus_copies = [], []
    for h in range(2):
        mate_copies[0][h].wait_recv()
        comb_out[0, h] = (sums[1, :, columns[h]] + mate_in[0, h].astype(F32)).astype(BF)
        minus_copies.append(send(comb_out.at[0, h], comb_in.at[0, h], k_minus))
        mate_copies[1][h].wait_recv()
        comb_out[1, h] = (sums[5, :, columns[h]] + mate_in[1, h].astype(F32)).astype(BF)
        plus_copies.append(send(comb_out.at[1, h], comb_in.at[1, h], k_plus))
        if h == 0:
            value = last_value(1 - 2 * core).astype(BF)
            for part in range(2):
                mate_out[2, part] = value[:, columns[part]]
                mate_copies[2].append(send(mate_out.at[2, part], mate_in.at[2, part], mate))
    sums[3] = last_value(0) + xblk[0].astype(F32)

    up_copy.wait()
    weight = weight_ref[...]
    g_plus, g_minus, g_mate, g_single = [], [], [], []
    kept = []
    for h in range(2):
        norm_h = norm[:, columns[h]]
        mate_copies[2][h].wait_recv()
        single_copies[h].wait_recv()
        total = sums[3, :, columns[h]] + mate_in[2, h].astype(F32) + comb_in[2, h].astype(F32)
        minus_copies[h].wait_recv()
        plus_copies[h].wait_recv()
        total = total + comb_in[0, h].astype(F32) + comb_in[1, h].astype(F32)
        aggregated = (norm_h * total).astype(BF)
        pre_act = (
            lax.dot_general(
                aggregated, weight, (((0,), (0,)), ((), ())), preferred_element_type=F32
            )
            + bias_ref[...]
        )
        gate = 1.0 / (1.0 + jnp.exp(-pre_act))
        rows = slice(h * HALF, (h + 1) * HALF)
        pre_grad = (
            up_v[rows, :].astype(F32) * (gate + pre_act * gate * (1.0 - gate))
        ).astype(BF)
        gblk[3, h] = (
            norm_h
            * lax.dot_general(
                weight, pre_grad, (((1,), (1,)), ((), ())), preferred_element_type=F32
            )
        ).astype(BF)
        g_plus.append(send(gblk.at[3, h], gblk.at[1, h], k_plus))
        g_minus.append(send(gblk.at[3, h], gblk.at[5, h], k_minus))
        g_mate.append(send(gblk.at[3, h], gblk.at[2 + 2 * core, h], mate))
        g_single.append(send(gblk.at[3, h], gblk.at[6 - 6 * core, h], single))
        hidden_v[rows, :] = (pre_act * gate).astype(BF)
        kept.append((aggregated, pre_grad))

    hidden_copy = pltpu.make_async_copy(hidden_v, hidden_hbm, local_sem.at[4])
    hidden_copy.start()
    local_weight = sum(jnp.dot(a, p, preferred_element_type=F32) for a, p in kept)
    local_bias = sum(jnp.sum(p.astype(F32), axis=0, keepdims=True) for _, p in kept)
    for i in range(4):
        for u in range(8):
            row = i * 32 + (u // 2) * 8
            lanes = slice((u % 2) * 128, (u % 2) * 128 + 128)
            w_send[i, u, 0:8] = local_weight[row : row + 8, lanes]
            w_send[i, u, 8:16] = jnp.broadcast_to(local_bias[:, lanes], (8, 128))
    w_y_copies = [
        send(w_send.at[lax.rem(y + j, 4)], w_y.at[y], y_peers[j - 1]) for j in range(1, 4)
    ]
    w_y[y] = w_send[y]

    def grad_product(source, groups):
        lhs = jnp.concatenate([gblk[g, h] for g in groups for h in range(2)], axis=1)
        rhs = jnp.concatenate(
            [
                jnp.concatenate(
                    [tile_v[table_s[g, a * 32 + source * 4 + b]] for b in range(4)], axis=1
                )
                for g in groups
                for a in range(4)
            ],
            axis=0,
        )
        return jnp.dot(lhs, rhs, preferred_element_type=F32)

    arrived(g_mate)
    for slot in range(8):
        sums[slot] = grad_product(source_block(slot), (3, 4 - 2 * core))
    arrived(w_y_copies)
    w_z[...] = w_y[0] + w_y[1] + w_y[2] + w_y[3]
    w_z_copies = [
        send(w_z.at[lax.rem(z + j, 8)], w_zin.at[j - 1], z_peers[j - 1]) for j in range(1, 8)
    ]
    passed = []
    for h in range(2):
        g_plus[h].wait_recv()
        passed.append(send(gblk.at[1, h], gblk.at[2 * core, h], mate))
        g_minus[h].wait_recv()
        passed.append(send(gblk.at[5, h], gblk.at[4 + 2 * core, h], mate))
    for slot in range(8):
        sums[slot] = sums[slot] + grad_product(source_block(slot), (1, 5))
    arrived(g_single + passed)

    def last_grad(slot):
        rest = (2 - 2 * core, 6 - 2 * core, 6 * core)
        return sums[slot] + grad_product(source_block(slot), rest)

    def first_hop(part):
        col_out[part, 2] = last_grad(part * 4 + 2).astype(BF)
        source = col_out.at[part, 2]
        to_plus = [send(source.at[low[i]], col_mid.at[part, 0, i], y_plus) for i in range(2)]
        to_minus = [send(source.at[high[i]], col_mid.at[part, 1, i], y_minus) for i in range(2)]
        return to_plus, to_minus

    def direct_hop(part):
        col_out[part, 1, FEAT // 2 :] = sums[part * 4 + 1, FEAT // 2 :].astype(BF)
        plus_b = send_parts(col_out.at[part, 1], col_in.at[part, 0], high, y_plus)
        col_out[part, 3, : FEAT // 2] = sums[part * 4 + 3, : FEAT // 2].astype(BF)
        minus_a = send_parts(col_out.at[part, 3], col_in.at[part, 1], low, y_minus)
        return plus_b, minus_a

    def relay_hop(part, to_plus, to_minus):
        plus_a, minus_b = [], []
        for i in range(2):
            to_plus[i].wait_recv()
            col_out[part, 1, low[i]] = (
                sums[part * 4 + 1, low[i]] + col_mid[part, 0, i].astype(F32)
            ).astype(BF)
            plus_a.append(
                send(col_out.at[part, 1, low[i]], col_in.at[part, 0, low[i]], y_plus)
            )
            to_minus[i].wait_recv()
            col_out[part, 3, high[i]] = (
                sums[part * 4 + 3, high[i]] + col_mid[part, 1, i].astype(F32)
            ).astype(BF)
            minus_b.append(
                send(col_out.at[part, 3, high[i]], col_in.at[part, 1, high[i]], y_minus)
            )
        return plus_a, minus_b

    far_first = first_hop(1)
    for slot in (5, 7):
        sums[slot] = last_grad(slot)
    far_plus_b, far_minus_a = direct_hop(1)
    for slot in (4, 1, 3):
        sums[slot] = last_grad(slot)
    arrived(w_z_copies)
    w_sum = w_z[z]
    for j in range(7):
        w_sum = w_sum + w_zin[j]
    w_x[...] = w_sum
    w_xall[x_place] = w_sum
    w_x_copies = [send(w_x, w_xall.at[x_place], x_peers[j - 1]) for j in range(1, 8)]
    far_plus_a, far_minus_b = relay_hop(1, *far_first)
    near_first = first_hop(0)
    near_plus_b, near_minus_a = direct_hop(0)
    own_grad = jnp.concatenate([gblk[3, 0], gblk[3, 1]], axis=1)
    sums[0] = last_grad(0) + own_grad.astype(F32)

    arrived(w_x_copies)
    w_sum = w_xall[0]
    for j in range(1, 8):
        w_sum = w_sum + w_xall[j]
    w_x_total[...] = w_sum
    w_zall[z] = w_sum
    w_g_copies = [send(w_x_total, w_zall.at[z], z_peers[j - 1]) for j in range(1, 8)]

    def partner_sum(part):
        xsum[part] = (
            sums[4, part] + col_in[1, 0, part].astype(F32) + col_in[1, 1, part].astype(F32)
        ).astype(BF)

    arrived(far_plus_b + far_minus_a)
    xs_a, xs_b = [], []
    for i in range(2):
        far_plus_a[i].wait_recv()
        partner_sum(low[i])
        xs_a.append(send(xsum.at[low[i]], xsum_in.at[low[i]], partner))
        far_minus_b[i].wait_recv()
        partner_sum(high[i])
        xs_b.append(send(xsum.at[high[i]], xsum_in.at[high[i]], partner))
    near_plus_a, near_minus_b = relay_hop(0, *near_first)
    arrived(w_g_copies)
    w_f_copies = [
        send(w_zall.at[:, pl.ds(0, 8)], w_all.at[y], y_peers[j - 1]) for j in range(1, 4)
    ]
    w_all[y] = w_zall[:, 0:8]
    scale = NODES ** (-0.5)
    bgrad_ref[:, 0:128] = w_zall[0, 8:9] * scale
    bgrad_ref[:, 128:256] = w_zall[1, 8:9] * scale
    arrived(near_plus_b + near_minus_a + near_plus_a + near_minus_b)
    column = sums[0] + col_in[0, 0].astype(F32) + col_in[0, 1].astype(F32)
    arrived(w_f_copies)
    for i in range(4):
        for u in range(8):
            row = i * 32 + (u // 2) * 8
            lane = (u % 2) * 128
            wgrad_ref[row : row + 8, lane : lane + 128] = w_all[i, u] * scale
    arrived(xs_a + xs_b)
    feature_grad = norm * (column + xsum_in[...].astype(F32))
    for i in range(4):
        fgrad_ref[i * TS : (i + 1) * TS, :] = feature_grad[:, i * TS : (i + 1) * TS].T.astype(BF)
    hidden_copy.wait()
    for copy in started:
        copy.wait_send()


def settle(*refs):
    in_sem, out_sem = refs[12:]
    loads = [pltpu.make_async_copy(refs[i], refs[8 + i], in_sem.at[i]) for i in range(4)]
    stores = [pltpu.make_async_copy(refs[8 + i], refs[4 + i], out_sem.at[i]) for i in range(4)]
    for load in loads:
        load.start()
    for load, store in zip(loads, stores):
        load.wait()
        store.start()
    for store in stores:
        store.wait()


def on_device(
    features, degrees, tile_weights, tile_rows, tile_cols, tile_counts, weight, layer_bias, upstream
):
    vmem = pl.BlockSpec(memory_space=pltpu.VMEM)
    smem = pl.BlockSpec(memory_space=pltpu.SMEM)
    anywhere = pl.BlockSpec(memory_space=pl.ANY)
    blocks = lambda *lead: pltpu.VMEM((*lead, FEAT, ROWS), BF)
    parts = lambda *lead: pltpu.VMEM((*lead, 2, FEAT, HALF), BF)
    quarters = lambda *lead: pltpu.VMEM((*lead, QUARTER, ROWS), BF)
    units = lambda *lead: pltpu.VMEM((*lead, 16, 128), F32)
    shapes = [
        jax.ShapeDtypeStruct((ROWS, HID), BF),
        jax.ShapeDtypeStruct((ROWS, FEAT), BF),
        jax.ShapeDtypeStruct((FEAT, HID), F32),
        jax.ShapeDtypeStruct((1, HID), F32),
    ]
    results = pl.pallas_call(
        kernel,
        in_specs=[smem, smem, anywhere, anywhere, vmem, anywhere, vmem, vmem, anywhere],
        out_specs=[anywhere, vmem, vmem, vmem],
        out_shape=shapes,
        scratch_shapes=[
            pltpu.VMEM((ROWS, HID), BF),
            pltpu.VMEM((ROWS, FEAT), BF),
            pltpu.VMEM((ROWS, HID), BF),
            pltpu.VMEM((SLOTS + 1, TS, TS), BF),
            pltpu.VMEM((SLOTS + 1, TS, TS), BF),
            pltpu.VMEM((8, FEAT, ROWS), F32),
            blocks(8),
            parts(3),
            parts(3),
            parts(3),
            parts(3),
            parts(7),
            blocks(2, 4),
            quarters(2, 2, 2),
            blocks(2, 2),
            blocks(),
            blocks(),
            units(4, 8),
            units(4, 8),
            units(8),
            units(7),
            units(),
            units(8),
            units(),
            units(8),
            pltpu.VMEM((4, 8, 8, 128), F32),
            pltpu.VMEM((8, 128), jnp.int32),
            pltpu.SMEM((8, 128), jnp.int32),
            pltpu.SMEM((1, 1), jnp.int32),
            pltpu.SemaphoreType.DMA((5,)),
            pltpu.SemaphoreType.DMA((CHUNKS,)),
            pltpu.SemaphoreType.DMA((N_COPIES,)),
            pltpu.SemaphoreType.DMA((N_COPIES,)),
        ],
        compiler_params=pltpu.CompilerParams(
            collective_id=0, has_side_effects=True, vmem_limit_bytes=56 << 20
        ),
        name="layer",
    )(
        tile_rows,
        tile_cols,
        tile_counts,
        features,
        degrees.reshape(1, ROWS),
        tile_weights.reshape(SLOTS, TS, TS),
        weight,
        layer_bias.reshape(1, HID),
        upstream,
    )
    hidden, feature_grad, weight_grad, bias_grad = pl.pallas_call(
        settle,
        in_specs=[anywhere] * 4,
        out_specs=[anywhere] * 4,
        out_shape=shapes,
        scratch_shapes=[pltpu.VMEM(shape.shape, shape.dtype) for shape in shapes]
        + [pltpu.SemaphoreType.DMA((4,)), pltpu.SemaphoreType.DMA((4,))],
        name="settle",
    )(*results)
    return hidden, feature_grad, weight_grad, bias_grad.reshape(HID)


def solution(mesh):
    placed = (
        P(("rep", "blk"), None),
        P(("rep", "blk")),
        P("rep", "blk", None, None, None),
        P("rep", "blk", None),
        P("rep", "blk", None),
        P("rep", "blk"),
        P(),
        P(),
        P(("rep", "blk"), None),
    )
    return jax.shard_map(
        on_device,
        mesh=mesh,
        in_specs=placed,
        out_specs=(P(("rep", "blk"), None), P(("rep", "blk"), None), P(), P()),
        check_vma=False,
    )
```
